512 devices in a mesh: shard: 128 (over y, z, core), rep: 4 (over x).
Axes of the slice: x: 4, y: 4, z: 16, core: 2. Of those that a mesh axis runs over, the one named last changes fastest.
Arguments:
- feature_table: bfloat16 [32768, 1024], P('shard'), may hold values from -8 to 8
- projection: bfloat16 [1024, 1024], replicated, may hold values from -0.1875 to 0.1875
- slot_owner: int32 [16384, 16, 1], P(('shard', 'rep')), may hold values from 0 to 127; in each aligned block of 512 rows (0 to 511, 512 to 1023, ..., all dimensions but the last counted through in order) at most 8 rows name the same one
- slot_row: int32 [16384, 16], P(('shard', 'rep')), may hold values from 0 to 255
- visits: int32 [16384, 13], P(('shard', 'rep')), may hold values from 1 to 32
- neg_row: int32 [512], P('shard'), may hold values from 0 to 255
Outputs:
- table_grad: float32 [32768, 1024], P('shard')
The draws below stay inside these ranges and needn't reach their ends.
Inputs may be any that keep to these rules, and one draw needn't show every extreme that they name: `slot_owner`: within the slots of one device's 32 queries (aligned blocks of 512 slots in order), no shard index is named more than 8 times, a bound that some block reaches. `neg_row`: negative j lies in the rows of shard index j // 4.
All inputs are finite; a program needn't handle non-finite values.
Results may differ from the reference program's by a relative error of at most 0.006.
Values may be sent and summed in bfloat16 or wider, within the bound.
No kernel may reach another device: no remote copies, remote signals or barrier semaphores. Data moves between devices by JAX's collectives and lax.ppermute only.
A program may use at most 64 MiB of HBM per device.

```python
import math
import jax
import jax.numpy as jnp
import numpy as np
from jax import lax

F = 1024
E = 1024
ROWS_DEV = 256
Q_DEV = 32
SLOTS = 16
NEG = 512
NODES = 32768
QUERIES = 16384
CAP = 8
NEG_DEV = 4
N_SHARD = 128


group_total = 16


def draw_feature_table(key, part):
    base = jax.random.fold_in(key, 4111)
    keys = jax.random.split(base, 2)
    member = jnp.arange(NODES, dtype=jnp.int32) % group_total
    centres = jax.random.normal(keys[0], (group_total, F), jnp.float32)
    noise = jax.random.normal(keys[1], (NODES, F), jnp.float32)
    table = centres[member] + noise
    return jnp.clip(table, -8.0, 8.0).astype(jnp.bfloat16)


def draw_slot_row(key, part):
    base = jax.random.fold_in(key, 7237)
    keys = jax.random.split(base, 6)
    span = ROWS_DEV // group_total
    home = jax.random.randint(keys[0], (QUERIES, 1), 0, group_total)
    first = jax.random.randint(keys[1], (QUERIES, SLOTS), 0, span)
    second = jax.random.randint(keys[2], (QUERIES, SLOTS), 0, span)
    within = jnp.minimum(first, second)
    stray = jax.random.randint(keys[3], (QUERIES, SLOTS), 0, group_total)
    stays = jax.random.randint(keys[4], (QUERIES, SLOTS), 0, 4) > 0
    offset = jax.random.randint(keys[5], (QUERIES, 1), 1, group_total)
    slot_index = jnp.arange(SLOTS, dtype=jnp.int32)[None, :]
    member = jnp.where(slot_index < 2, home, jnp.where(slot_index == 2, (home + offset) % group_total, jnp.where(stays, home, stray)))
    return (within * group_total + member).astype(jnp.int32)


def plant(result, own_key, smallest, largest):
    extent = result.shape
    place = [jax.random.randint(jax.random.fold_in(own_key, axis), (), 0, extent[axis]) for axis in range(len(extent))]
    result = result.at[tuple(place)].set(smallest)
    longest = extent.index(max(extent))
    place[longest] = (place[longest] + 1) % extent[longest]
    return result.at[tuple(place)].set(largest)


def routed_block(rng, own, number, rows, number_of, top, bound, lean):
    ranking = jax.random.permutation(rng, number_of)
    packed, common = shares(number_of, rows * top, bound, lean, True), shares(number_of, rows * top, bound, lean, False)
    places = jnp.arange(number_of)

    def named(tallies, rotation):
        used = int((tallies > 0).sum())
        fixed = max(1, used // 4)
        passed = fixed + (places - fixed + rotation * (used - fixed)) % max(1, number_of - fixed)
        return jnp.zeros((number_of,), jnp.int32).at[ranking[jnp.where(places < fixed, places, passed)]].set(jnp.asarray(tallies, jnp.int32))

    tallies = jnp.where(number % 4 == 0, named(packed, number // 4), named(common, number - number // 4 - 1))
    mixed = jax.random.permutation(jax.random.fold_in(own, 3), number_of)
    giver, taker = mixed[0:number_of // 2 * 2:2], mixed[1:number_of // 2 * 2:2]
    room = jnp.minimum(tallies[giver] - 1, bound - tallies[taker]) // 2
    room = jnp.where((giver == ranking[0]) | (taker == ranking[0]) | (tallies[taker] == 0), 0, jnp.maximum(room, 0))
    passed = jax.random.randint(jax.random.fold_in(own, 4), (number_of // 2,), 0, 1 << 20) % (room + 1)
    tallies = tallies.at[giver].add(-passed).at[taker].add(passed)
    members = jnp.searchsorted(jnp.cumsum(tallies), jnp.arange(rows * top), side="right").astype(jnp.int32)
    table = members.reshape(top, rows).T
    table = table[jax.random.permutation(jax.random.fold_in(own, 1), rows)]
    rotation = jax.random.randint(jax.random.fold_in(own, 2), (rows, 1), 0, top)
    return jnp.take_along_axis(table, (jnp.arange(top)[None, :] + rotation) % top, axis=1)


def shares(amount, total, bound, lean, full):
    weights = [(1 << 20) // math.isqrt(grade ** lean) + 1 for grade in range(1, amount + 1)]
    largest = bound if full else min(bound, max(-(-total // amount), total * weights[0] // sum(weights)))
    least = 1 if total - largest >= amount - 1 else 0
    counts, surplus = [largest] + [least] * (amount - 1), total - largest - least * (amount - 1)
    while surplus > 0:
        candidates = [i for i in range(1, amount) if counts[i] < largest] or [i for i in range(1, amount) if counts[i] < bound]
        pool, left = sum([weights[i] for i in candidates]), surplus
        for i in candidates:
            extra = min(bound - counts[i], max(1, left * weights[i] // pool), surplus)
            counts[i] = counts[i] + extra
            surplus = surplus - extra
    return np.array(counts)


def bell_draw(key, dims, deviation, limit, kind=jnp.bfloat16):
    array = deviation * jax.random.normal(key, dims, jnp.float32)
    return jnp.clip(array, min=-limit, max=limit).astype(kind)


def setup_inputs(seed: int = 0) -> dict:
    splits = jax.random.split(jax.random.key(seed), 7)
    feature_table = draw_feature_table(jax.random.fold_in(splits[6], 71), 0)
    projection = bell_draw(splits[1], (F, E), F ** -0.5, 0.1875)
    slot_owner_keys = jax.random.split(jax.random.fold_in(splits[2], 1), QUERIES * SLOTS // (Q_DEV * SLOTS))
    slot_owner_turns = jax.random.permutation(jax.random.fold_in(splits[2], 3), QUERIES * SLOTS // (Q_DEV * SLOTS))
    slot_owner = jax.vmap(lambda own, number: routed_block(jax.random.fold_in(splits[2], 2), own, number, Q_DEV * SLOTS, N_SHARD, 1, CAP, 2))(slot_owner_keys, slot_owner_turns).reshape((QUERIES, SLOTS, 1))
    slot_row = draw_slot_row(jax.random.fold_in(splits[6], 71), 0)
    visits = plant(jax.random.randint(splits[4], (QUERIES, SLOTS - 3), 1, 33), jax.random.fold_in(splits[4], 1), 1, 32).astype(jnp.int32)
    neg_row = plant(jax.random.randint(splits[5], (NEG,), 0, ROWS_DEV), jax.random.fold_in(splits[5], 1), 0, ROWS_DEV - 1).astype(jnp.int32)
    return {"feature_table": feature_table, "projection": projection, "slot_owner": slot_owner, "slot_row": slot_row, "visits": visits, "neg_row": neg_row}


score_scale = 8.0
margin_value = 0.1
epsilon = 1e-06

def unit_rows(values):
    norms = jnp.sqrt(lax.optimization_barrier(jnp.sum(values * values, axis=-1, keepdims=True)) + epsilon)
    return (values / norms, norms)

def unit_back(grads, unit, norms):
    return (grads - unit * lax.optimization_barrier(jnp.sum(unit * grads, axis=-1, keepdims=True))) / norms

def silu_slope(preact):
    gate_value = jax.nn.sigmoid(preact)
    return gate_value * (1.0 + preact * (1.0 - gate_value))

def reference(feature_table, projection, slot_owner, slot_row, visits, neg_row):
    node_ids = (slot_owner[:, :, 0] * ROWS_DEV + slot_row).astype(jnp.int32)
    neg_ids = (jnp.arange(NEG, dtype=jnp.int32) // NEG_DEV * ROWS_DEV + neg_row).astype(jnp.int32)
    neg_pre = jnp.dot(feature_table[neg_ids], projection, preferred_element_type=jnp.float32)
    neg_unit, neg_norms = unit_rows(jax.nn.silu(neg_pre))
    neg_embed = neg_unit.astype(jnp.bfloat16)
    visit_float = visits.astype(jnp.float32)
    coefs = visit_float / lax.optimization_barrier(jnp.sum(visit_float, axis=1, keepdims=True))
    block = min(QUERIES, 256)
    block_count = QUERIES // block
    node_blocks = node_ids.reshape(block_count, block, SLOTS)
    coef_blocks = coefs.reshape(block_count, block, SLOTS - 3)

    def visit_block(carry, inputs):
        grad_table, neg_grad = carry
        block_nodes, block_coefs = inputs
        gathered = feature_table[block_nodes.reshape(-1)]
        preact = jnp.dot(gathered, projection, preferred_element_type=jnp.float32).reshape(block, SLOTS, E)
        active = jax.nn.silu(preact)
        hood = active[:, 0] + jnp.einsum('bk,bke->be', block_coefs, active[:, 3:])
        query_unit, query_norms = unit_rows(hood)
        query_embed = query_unit.astype(jnp.bfloat16)
        item_unit, item_norms = unit_rows(active[:, 1:3])
        item_embed = item_unit.astype(jnp.bfloat16)
        query_float = query_embed.astype(jnp.float32)
        item_float = item_embed.astype(jnp.float32)
        neg_scores = jnp.dot(query_embed, neg_embed.T, preferred_element_type=jnp.float32)
        pair_scores = jnp.einsum('be,bse->bs', query_float, item_float)
        positive = pair_scores[:, 0:1]
        neg_weight = (score_scale * jax.nn.sigmoid(score_scale * (neg_scores - positive + margin_value))).astype(jnp.bfloat16)
        hard_weight = (score_scale * jax.nn.sigmoid(score_scale * (pair_scores[:, 1:2] - positive + margin_value))).astype(jnp.bfloat16)
        hard_float = hard_weight.astype(jnp.float32)
        total_weight = lax.optimization_barrier(jnp.sum(neg_weight.astype(jnp.float32), axis=1, keepdims=True)) + hard_float
        query_grad = jnp.dot(neg_weight, neg_embed, preferred_element_type=jnp.float32) + hard_float * item_float[:, 1] - total_weight * item_float[:, 0]
        item_grad = jnp.stack([-total_weight * query_float, hard_float * query_float], axis=1)
        neg_grad = neg_grad + jnp.dot(neg_weight.T, query_embed, preferred_element_type=jnp.float32)
        hood_grad = unit_back(query_grad, query_unit, query_norms)
        item_back = unit_back(item_grad, item_unit, item_norms)
        active_grad = jnp.concatenate([hood_grad[:, None], item_back, block_coefs[:, :, None] * hood_grad[:, None]], axis=1)
        preact_grad = (active_grad * silu_slope(preact)).astype(jnp.bfloat16)
        row_grads = jnp.dot(preact_grad.reshape(block * SLOTS, E), projection.T, preferred_element_type=jnp.float32)
        grad_table = grad_table.at[block_nodes.reshape(-1)].add(row_grads)
        return ((grad_table, neg_grad), None)
    start = (jnp.zeros((NODES, F), jnp.float32), jnp.zeros((NEG, E), jnp.float32))
    (grad_table, neg_grad), unused = lax.scan(visit_block, start, (node_blocks, coef_blocks))
    neg_back = unit_back(neg_grad, neg_unit, neg_norms)
    neg_pre_grad = (neg_back * silu_slope(neg_pre)).astype(jnp.bfloat16)
    neg_rows = jnp.dot(neg_pre_grad, projection.T, preferred_element_type=jnp.float32)
    return grad_table.at[neg_ids].add(neg_rows)
```

```python
import jax
import jax.numpy as jnp
from jax import lax
from jax.sharding import Mesh
from jax.sharding import PartitionSpec as P

score_scale = 8.0
margin_value = 0.1
epsilon = 1e-06

Y, Z, C, X = 4, 16, 2, 4
ROWS = 256
PART = ROWS // X
BLOCK = PART + 8
OWN = X * BLOCK
bf16 = jnp.bfloat16
f32 = jnp.float32


def unit_rows(values):
    norms = jnp.sqrt(jnp.sum(values * values, axis=-1, keepdims=True) + epsilon)
    return (values / norms, norms)


def unit_back(grads, unit, norms):
    return (grads - unit * jnp.sum(unit * grads, axis=-1, keepdims=True)) / norms


def silu_slope(preact):
    gate_value = jax.nn.sigmoid(preact)
    return gate_value * (1.0 + preact * (1.0 - gate_value))


def weigh(score, positive):
    return (score_scale * jax.nn.sigmoid(score_scale * (score - positive + margin_value))).astype(bf16)


def dot_f32(left, right, dims):
    return lax.dot_general(left, right, (dims, ((), ())), preferred_element_type=f32)


def decode(packed, z):
    owner = packed & 127
    row = (packed >> 7) & 255
    visits = (packed >> 15).astype(f32)
    coefs = visits / jnp.sum(visits, axis=1, keepdims=True)
    place = (row // PART) * BLOCK + row % PART
    here = ((owner // C) % Z) == z
    return owner // (C * Z), owner % C, place, here, coefs


def hot_rows(column, coefs, width):
    lanes = lax.broadcasted_iota(jnp.int32, (column.shape[0], width), 1)
    total = (column[:, 0:1] == lanes).astype(f32)
    for slot in range(3, column.shape[1]):
        total = total + jnp.where(column[:, slot : slot + 1] == lanes, coefs[:, slot : slot + 1], 0.0)
    first = (column[:, 1:2] == lanes).astype(bf16)
    second = (column[:, 2:3] == lanes).astype(bf16)
    return lax.optimization_barrier((total.astype(bf16), first, second))


def on_device(feature_table, projection, slot_owner, slot_row, visits, neg_row):
    y, z, c, x = (lax.axis_index(a) for a in ("y", "z", "c", "x"))
    query_count, slot_count = slot_row.shape
    feat_width, embed_width = projection.shape
    line_count = Z * query_count

    shifted = jnp.pad(visits, ((0, 0), (3, 0)))
    packed = slot_owner.reshape(query_count, slot_count) + slot_row * 128 + shifted * 32768

    rows = jnp.concatenate(
        [
            feature_table.reshape(X, PART, feat_width),
            feature_table[neg_row].reshape(X, 1, feat_width),
            jnp.zeros((X, BLOCK - PART - 1, feat_width), bf16),
        ],
        axis=1,
    ).reshape(OWN, feat_width)
    pre = jnp.dot(rows, projection, preferred_element_type=f32)
    act = jax.nn.silu(pre)
    act_norm = jnp.sqrt(jnp.sum(act * act, axis=1, keepdims=True) + epsilon)
    is_neg = (lax.broadcasted_iota(jnp.int32, (OWN, 1), 0) % BLOCK) == PART
    shared = (act / jnp.where(is_neg, act_norm, 1.0)).astype(bf16)
    plane = lax.all_gather(shared, ("y", "c"), axis=0, tiled=True)

    line = lax.all_gather(packed, "z", axis=0, tiled=True)
    line_sib = lax.ppermute(line, "c", [(0, 1), (1, 0)])
    ny, nc, place, here, coefs = decode(line, z)
    column = jnp.where(here, (ny * C + nc) * OWN + place, -1)
    hood_w, first, second = hot_rows(column, coefs, Y * C * OWN)

    def fold(v):
        return v.reshape(Z, query_count, v.shape[-1])

    spread = jnp.stack([fold(hood_w), fold(first), fold(second)], axis=1).reshape(3 * line_count, -1)
    part = jnp.dot(spread, plane, preferred_element_type=f32).astype(bf16)
    got = lax.psum_scatter(part, "z", scatter_dimension=0, tiled=True)

    plane_neg = plane.reshape(Y, C, X, BLOCK, embed_width)[:, :, :, PART]
    half_neg = lax.dynamic_index_in_dim(plane_neg, c, axis=1, keepdims=False).reshape(Y * X, embed_width)
    some_neg = lax.all_gather(half_neg, "z", axis=0, tiled=True)
    other_neg = lax.ppermute(some_neg, "c", [(0, 1), (1, 0)])
    neg_embed = jnp.concatenate([some_neg, other_neg], axis=0)

    got = got.astype(f32)
    hood = got[:query_count]
    items = jnp.stack([got[query_count : 2 * query_count], got[2 * query_count :]], axis=1)
    query_unit, query_norms = unit_rows(hood)
    query_embed = query_unit.astype(bf16)
    item_unit, item_norms = unit_rows(items)
    query_float = query_embed.astype(f32)
    item_float = item_unit.astype(bf16).astype(f32)
    neg_scores = dot_f32(query_embed, neg_embed, ((1,), (1,)))
    pair_scores = jnp.sum(query_float[:, None, :] * item_float, axis=2)
    positive = pair_scores[:, 0:1]
    neg_weight = weigh(neg_scores, positive)
    hard_float = weigh(pair_scores[:, 1:2], positive).astype(f32)
    total_weight = jnp.sum(neg_weight.astype(f32), axis=1, keepdims=True) + hard_float
    query_grad = (
        jnp.dot(neg_weight, neg_embed, preferred_element_type=f32)
        + hard_float * item_float[:, 1]
        - total_weight * item_float[:, 0]
    )
    hood_grad = unit_back(query_grad, query_unit, query_norms).astype(bf16)
    item_weight = jnp.concatenate([-total_weight, hard_float], axis=1)
    overlap = jnp.sum(query_float[:, None, :] * item_unit, axis=2)
    on_query = item_weight / item_norms[:, :, 0]
    on_act = -item_weight * overlap / (item_norms[:, :, 0] * item_norms[:, :, 0])
    scalars = jnp.concatenate([on_query, on_act, positive, jnp.zeros((query_count, 3), f32)], axis=1)

    vectors = lax.all_gather(jnp.concatenate([hood_grad, query_embed], axis=0), "z", axis=0, tiled=True)
    scal = lax.all_gather(scalars, "z", axis=0, tiled=True)
    scal_sib = lax.ppermute(scal, "c", [(0, 1), (1, 0)])
    vectors_sib = lax.ppermute(vectors, "c", [(0, 1), (1, 0)])

    core_plane = lax.dynamic_index_in_dim(plane.reshape(Y, C, OWN, embed_width), c, axis=1, keepdims=False)
    core_plane = core_plane.reshape(Y * OWN, embed_width)
    core_neg = half_neg
    width = Y * OWN
    neg_spot = (
        lax.broadcasted_iota(jnp.int32, (Y * X, width), 0) * BLOCK + PART
        == lax.broadcasted_iota(jnp.int32, (Y * X, width), 1)
    ).astype(bf16)

    def to_nodes(packed_line, vecs, scals):
        ly, lc, lplace, lhere, lcoefs = decode(packed_line, z)
        lcolumn = jnp.where(lhere & (lc == c), ly * OWN + lplace, -1)
        w_hood, w_first, w_second = hot_rows(lcolumn, lcoefs, width)
        scores = dot_f32(vecs, core_neg, ((1,), (1,))).reshape(Z, 2, query_count, Y * X)[:, 1]
        neg_w = weigh(scores.reshape(line_count, Y * X), scals[:, 4:5])
        w_query = (
            w_first.astype(f32) * scals[:, 0:1]
            + w_second.astype(f32) * scals[:, 1:2]
            + jnp.dot(neg_w, neg_spot, preferred_element_type=f32)
        ).astype(bf16)
        both = jnp.stack([fold(w_hood), fold(w_query)], axis=1).reshape(2 * line_count, width)
        grads = dot_f32(both, vecs, ((0,), (0,)))
        on_acts = dot_f32(w_first, scals[:, 2:3].astype(bf16), ((0,), (0,))) + dot_f32(
            w_second, scals[:, 3:4].astype(bf16), ((0,), (0,))
        )
        return grads, on_acts

    grads, on_acts = to_nodes(line, vectors, scal)
    grads_sib, on_acts_sib = to_nodes(line_sib, vectors_sib, scal_sib)
    node_grads = grads + grads_sib + (on_acts + on_acts_sib) * core_plane.astype(f32)

    pieces = lax.all_to_all(node_grads.astype(bf16), ("y", "x"), split_axis=0, concat_axis=0, tiled=True)
    mine = jnp.sum(pieces.reshape(Y * X, BLOCK, embed_width).astype(f32), axis=0)
    my_pre = lax.dynamic_slice_in_dim(pre, x * BLOCK, BLOCK, axis=0)
    my_unit, my_norms = unit_rows(jax.nn.silu(my_pre))
    row_is_neg = lax.broadcasted_iota(jnp.int32, (BLOCK, 1), 0) == PART
    mine = jnp.where(row_is_neg, unit_back(mine, my_unit, my_norms), mine)
    pre_grad = (mine * silu_slope(my_pre)).astype(bf16)
    all_pre_grad = lax.all_gather(pre_grad, "x", axis=0, tiled=True)
    out = dot_f32(all_pre_grad, projection, ((1,), (1,))).reshape(X, BLOCK, feat_width)
    result = out[:, :PART].reshape(ROWS, feat_width)
    row_ids = lax.broadcasted_iota(jnp.int32, (ROWS, 1), 0)
    for i in range(X):
        result = result + jnp.where(row_ids == neg_row[i], out[i, PART][None, :], 0.0)
    return result


def solution(mesh):
    grid = Mesh(mesh.devices.reshape(Y, Z, C, X), ("y", "z", "c", "x"))
    shard = ("y", "z", "c")
    every = ("y", "z", "c", "x")
    return jax.shard_map(
        on_device,
        mesh=grid,
        in_specs=(
            P(shard, None),
            P(),
            P(every, None, None),
            P(every, None),
            P(every, None),
            P(shard),
        ),
        out_specs=P(shard, None),
        check_vma=False,
    )
```

```python
import jax
import jax.numpy as jnp
from jax import lax
from jax.sharding import Mesh
from jax.sharding import PartitionSpec as P

score_scale = 8.0
margin_value = 0.1
epsilon = 1e-06

Y, Z, C, X = 4, 16, 2, 4
ROWS = 256
PART = ROWS // X
BLOCK = PART + 8
OWN = X * BLOCK
bf16 = jnp.bfloat16
f16 = jnp.float16
f32 = jnp.float32


def unit_rows(values):
    norms = jnp.sqrt(jnp.sum(values * values, axis=-1, keepdims=True) + epsilon)
    return (values / norms, norms)


def unit_back(grads, unit, norms):
    return (grads - unit * jnp.sum(unit * grads, axis=-1, keepdims=True)) / norms


def silu_slope(preact):
    gate_value = jax.nn.sigmoid(preact)
    return gate_value * (1.0 + preact * (1.0 - gate_value))


def weigh(score, positive):
    return (score_scale * jax.nn.sigmoid(score_scale * (score - positive + margin_value))).astype(bf16)


def dot_f32(left, right, dims):
    return lax.dot_general(left, right, (dims, ((), ())), preferred_element_type=f32)


def decode(packed, z):
    owner = packed & 127
    row = (packed >> 7) & 255
    visits = (packed >> 15).astype(f32)
    coefs = visits / jnp.sum(visits, axis=1, keepdims=True)
    place = (row // PART) * BLOCK + row % PART
    here = ((owner // C) % Z) == z
    return owner // (C * Z), owner % C, place, here, coefs


def hot_rows(column, coefs, width):
    lanes = lax.broadcasted_iota(jnp.int32, (column.shape[0], width), 1)
    total = (column[:, 0:1] == lanes).astype(f32)
    for slot in range(3, column.shape[1]):
        total = total + jnp.where(column[:, slot : slot + 1] == lanes, coefs[:, slot : slot + 1], 0.0)
    first = (column[:, 1:2] == lanes).astype(bf16)
    second = (column[:, 2:3] == lanes).astype(bf16)
    return lax.optimization_barrier((total.astype(bf16), first, second))


def on_device(feature_table, projection, slot_owner, slot_row, visits, neg_row):
    y, z, c, x = (lax.axis_index(a) for a in ("y", "z", "c", "x"))
    query_count, slot_count = slot_row.shape
    feat_width, embed_width = projection.shape
    line_count = Z * query_count

    shifted = jnp.pad(visits, ((0, 0), (3, 0)))
    packed = slot_owner.reshape(query_count, slot_count) + slot_row * 128 + shifted * 32768

    rows = jnp.concatenate(
        [
            feature_table.reshape(X, PART, feat_width),
            feature_table[neg_row].reshape(X, 1, feat_width),
            jnp.zeros((X, BLOCK - PART - 1, feat_width), bf16),
        ],
        axis=1,
    ).reshape(OWN, feat_width)
    pre = jnp.dot(rows, projection, preferred_element_type=f32)
    act = jax.nn.silu(pre)
    act_norm = jnp.sqrt(jnp.sum(act * act, axis=1, keepdims=True) + epsilon)
    is_neg = (lax.broadcasted_iota(jnp.int32, (OWN, 1), 0) % BLOCK) == PART
    shared = (act / jnp.where(is_neg, act_norm, 1.0)).astype(bf16)
    plane = lax.all_gather(shared, ("y", "c"), axis=0, tiled=True)

    line = lax.all_gather(packed, "z", axis=0, tiled=True)
    line_sib = lax.ppermute(line, "c", [(0, 1), (1, 0)])
    ny, nc, place, here, coefs = decode(line, z)
    column = jnp.where(here, (ny * C + nc) * OWN + place, -1)
    hood_w, first, second = hot_rows(column, coefs, Y * C * OWN)

    def fold(v):
        return v.reshape(Z, query_count, v.shape[-1])

    spread = jnp.stack([fold(hood_w), fold(first), fold(second)], axis=1).reshape(3 * line_count, -1)
    part = jnp.dot(spread, plane, preferred_element_type=f32).astype(bf16)
    got = lax.psum_scatter(part, "z", scatter_dimension=0, tiled=True)

    plane_neg = plane.reshape(Y, C, X, BLOCK, embed_width)[:, :, :, PART]
    half_neg = lax.dynamic_index_in_dim(plane_neg, c, axis=1, keepdims=False).reshape(Y * X, embed_width)
    some_neg = lax.all_gather(half_neg, "z", axis=0, tiled=True)
    other_neg = lax.ppermute(some_neg, "c", [(0, 1), (1, 0)])
    neg_embed = jnp.concatenate([some_neg, other_neg], axis=0)

    width = Y * OWN
    core_plane = lax.dynamic_index_in_dim(plane.reshape(Y, C, OWN, embed_width), c, axis=1, keepdims=False)
    core_plane = core_plane.reshape(width, embed_width)
    core_is_neg = (lax.broadcasted_iota(jnp.int32, (width, 1), 0) % BLOCK) == PART
    neg_spot = (
        lax.broadcasted_iota(jnp.int32, (Y * X, width), 0) * BLOCK + PART
        == lax.broadcasted_iota(jnp.int32, (Y * X, width), 1)
    ).astype(bf16)

    def core_rows(packed_line):
        ly, lc, lplace, lhere, lcoefs = decode(packed_line, z)
        return hot_rows(jnp.where(lhere & (lc == c), ly * OWN + lplace, -1), lcoefs, width)

    weights, weights_sib = core_rows(line), core_rows(line_sib)
    got, weights, weights_sib, core_plane, neg_embed = lax.optimization_barrier(
        (got, weights, weights_sib, core_plane, neg_embed)
    )

    got = got.astype(f32)
    hood = got[:query_count]
    items = jnp.stack([got[query_count : 2 * query_count], got[2 * query_count :]], axis=1)
    query_unit, query_norms = unit_rows(hood)
    query_embed = query_unit.astype(bf16)
    item_unit, item_norms = unit_rows(items)
    query_float = query_embed.astype(f32)
    item_float = item_unit.astype(bf16).astype(f32)
    neg_scores = dot_f32(query_embed, neg_embed, ((1,), (1,)))
    pair_scores = jnp.sum(query_float[:, None, :] * item_float, axis=2)
    positive = pair_scores[:, 0:1]
    neg_weight = weigh(neg_scores, positive)
    hard_float = weigh(pair_scores[:, 1:2], positive).astype(f32)
    total_weight = jnp.sum(neg_weight.astype(f32), axis=1, keepdims=True) + hard_float
    query_grad = (
        jnp.dot(neg_weight, neg_embed, preferred_element_type=f32)
        + hard_float * item_float[:, 1]
        - total_weight * item_float[:, 0]
    )
    query_grad = query_grad - query_unit * jnp.sum(query_unit * query_grad, axis=1, keepdims=True)
    lead = positive.astype(f16)
    scalars = jnp.concatenate(
        [
            -total_weight,
            hard_float,
            item_norms[:, :, 0],
            query_norms * 0.25,
            lead.astype(f32),
            positive - lead.astype(f32),
            jnp.zeros((query_count, 121), f32),
        ],
        axis=1,
    )
    payload = jnp.concatenate([query_grad, query_float, scalars], axis=1).astype(f16)
    vectors = lax.all_gather(payload, "z", axis=0, tiled=True)
    vectors_sib = lax.ppermute(vectors, "c", [(0, 1), (1, 0)])

    def unpack(vecs):
        scals = vecs[:, 2 * embed_width :].astype(f32)
        grads = (vecs[:, :embed_width].astype(f32) / (4.0 * scals[:, 4:5])).astype(bf16)
        embeds = vecs[:, embed_width : 2 * embed_width].astype(bf16)
        on_first = scals[:, 0:1] / scals[:, 2:3]
        on_second = scals[:, 1:2] / scals[:, 3:4]
        pos = scals[:, 5:6] + scals[:, 6:7]
        return lax.optimization_barrier((grads, embeds, jnp.concatenate([on_first, on_second, pos], axis=1)))

    def to_nodes(weights, received):
        w_hood, w_first, w_second = weights
        grads, embeds, scals = received
        scores = dot_f32(embeds, half_neg, ((1,), (1,)))
        neg_w = weigh(scores, scals[:, 2:3])
        w_query = (
            w_first.astype(f32) * scals[:, 0:1]
            + w_second.astype(f32) * scals[:, 1:2]
            + jnp.dot(neg_w, neg_spot, preferred_element_type=f32)
        ).astype(bf16)
        return dot_f32(w_hood, grads, ((0,), (0,))), dot_f32(w_query, embeds, ((0,), (0,)))

    own = unpack(vectors)
    hood_part, query_part = to_nodes(weights, own)
    hood_sib, query_sib = to_nodes(weights_sib, unpack(vectors_sib))
    query_part = query_part + query_sib
    core_float = core_plane.astype(f32)
    core_square = jnp.where(core_is_neg, 0.0, 1.0 / (jnp.sum(core_float * core_float, axis=1, keepdims=True) + epsilon))
    query_part = query_part - core_float * (core_square * jnp.sum(core_float * query_part, axis=1, keepdims=True))
    node_grads = (hood_part + hood_sib + query_part).astype(bf16)

    my_pre = lax.dynamic_slice_in_dim(pre, x * BLOCK, BLOCK, axis=0)
    my_unit, my_norms = unit_rows(jax.nn.silu(my_pre))
    my_slope = silu_slope(my_pre)
    node_grads, my_unit, my_norms, my_slope, nowhere = lax.optimization_barrier(
        (node_grads, my_unit, my_norms, my_slope, x * 0)
    )
    pieces = lax.all_to_all(node_grads, ("y", "x"), split_axis=0, concat_axis=0, tiled=True)
    pieces, neg_row, nowhere = lax.optimization_barrier((pieces, neg_row, nowhere))
    mine = jnp.sum(pieces.reshape(Y * X, BLOCK, embed_width).astype(f32), axis=0)
    row_is_neg = lax.broadcasted_iota(jnp.int32, (BLOCK, 1), 0) == PART + nowhere
    mine = jnp.where(row_is_neg, unit_back(mine, my_unit, my_norms), mine)
    pre_grad = (mine * my_slope).astype(bf16)
    all_pre_grad = lax.all_gather(pre_grad, "x", axis=0, tiled=True)
    out = dot_f32(all_pre_grad, projection, ((1,), (1,))).reshape(X, BLOCK, feat_width)
    result = out[:, :PART].reshape(ROWS, feat_width)
    row_ids = lax.broadcasted_iota(jnp.int32, (ROWS, 1), 0)
    for i in range(X):
        result = result + jnp.where(row_ids == neg_row[i], out[i, PART][None, :], 0.0)
    return result


def solution(mesh):
    grid = Mesh(mesh.devices.reshape(Y, Z, C, X), ("y", "z", "c", "x"))
    shard = ("y", "z", "c")
    every = ("y", "z", "c", "x")
    return jax.shard_map(
        on_device,
        mesh=grid,
        in_specs=(
            P(shard, None),
            P(),
            P(every, None, None),
            P(every, None),
            P(every, None),
            P(shard),
        ),
        out_specs=P(shard, None),
        check_vma=False,
    )
```

```python
import jax
import jax.numpy as jnp
from jax import lax
from jax.experimental import pallas as pl
from jax.experimental.pallas import tpu as pltpu
from jax.sharding import Mesh
from jax.sharding import PartitionSpec as P

score_scale = 8.0
margin_value = 0.1
epsilon = 1e-06
log_two = 0.6931471805599453

Y, Z, C, X = 4, 16, 2, 4
ROWS = 256
PART = ROWS // X
BLOCK = PART + 8
OWN = X * BLOCK
WIDE = Y * C * OWN
NARROW = Y * OWN
bf16 = jnp.bfloat16
f16 = jnp.float16
f32 = jnp.float32
SIBLING = [(0, 1), (1, 0)]


def silu_slope(preact):
    gate_value = jax.nn.sigmoid(preact)
    return gate_value * (1.0 + preact * (1.0 - gate_value))


def row_sum(values):
    return jnp.sum(values, axis=1, keepdims=True)


def row_norm(values):
    return jnp.sqrt(row_sum(values * values) + epsilon)


def weigh(score, positive):
    return (score_scale * jax.nn.sigmoid(score_scale * (score - positive + margin_value))).astype(bf16)


def dot_nn(left, right):
    return lax.dot_general(left, right, (((1,), (0,)), ((), ())), preferred_element_type=f32)


def dot_nt(left, right):
    return lax.dot_general(left, right, (((1,), (1,)), ((), ())), preferred_element_type=f32)


def decode(packed, axis):
    owner = packed & 127
    row = (packed >> 7) & 255
    visits = (packed >> 15).astype(f32)
    coefs = visits / jnp.sum(visits, axis=axis, keepdims=True)
    return owner >> 5, owner & 1, (owner >> 1) & 15, row >> 6, row & 63, coefs


def spread_kernel(where_ref, line_ref, out_ref):
    ny, nc, nz, part, rest, coefs = decode(line_ref[...], 1)
    column = jnp.where(nz == where_ref[0], (ny * C + nc) * OWN + part * BLOCK + rest, -1)
    rows, slots = column.shape
    chunk = WIDE // 3
    for k in range(3):
        lanes = lax.broadcasted_iota(jnp.int32, (rows, chunk), 1) + k * chunk
        total = jnp.where(lanes == column[:, 0:1], 1.0, 0.0)
        for slot in range(3, slots):
            total = total + jnp.where(lanes == column[:, slot : slot + 1], coefs[:, slot : slot + 1], 0.0)
        span = pl.ds(k * chunk, chunk)
        out_ref[0, 0, :, span] = total.astype(bf16)
        out_ref[0, 1, :, span] = jnp.where(lanes == column[:, 1:2], 1.0, 0.0).astype(bf16)
        out_ref[0, 2, :, span] = jnp.where(lanes == column[:, 2:3], 1.0, 0.0).astype(bf16)


def node_weights_kernel(where_ref, line_ref, out_ref):
    ny, nc, nz, part, rest, coefs = decode(line_ref[...], 0)
    here = (nz == where_ref[0]) & (nc == where_ref[1])
    column = jnp.where(here, part * (Y * BLOCK) + ny * BLOCK + rest, -1)
    slots, count = column.shape
    base = pl.program_id(0) * OWN
    chunk = 32
    for k in range(OWN // chunk):
        nodes = lax.broadcasted_iota(jnp.int32, (chunk, count), 0) + (base + k * chunk)
        total = jnp.where(nodes == column[0:1], 1.0, 0.0)
        for slot in range(3, slots):
            total = total + jnp.where(nodes == column[slot : slot + 1], coefs[slot : slot + 1], 0.0)
        span = pl.ds(k * chunk, chunk)
        out_ref[0, span, :] = total.astype(bf16)
        out_ref[1, span, :] = jnp.where(nodes == column[1:2], 1.0, 0.0).astype(bf16)
        out_ref[2, span, :] = jnp.where(nodes == column[2:3], 1.0, 0.0).astype(bf16)


def query_kernel(got_ref, neg_a_ref, neg_b_ref, out_ref):
    count = got_ref.shape[0] // 3
    width = got_ref.shape[1]
    hood = got_ref[0:count].astype(f32)
    query_norm = row_norm(hood)
    query_unit = hood / query_norm
    query_embed = query_unit.astype(bf16)
    query_float = query_embed.astype(f32)
    first = got_ref[count : 2 * count].astype(f32)
    second = got_ref[2 * count :].astype(f32)
    first_norm, second_norm = row_norm(first), row_norm(second)
    first_embed = (first / first_norm).astype(bf16).astype(f32)
    second_embed = (second / second_norm).astype(bf16).astype(f32)
    positive = row_sum(query_float * first_embed)
    hard = weigh(row_sum(query_float * second_embed), positive).astype(f32)
    weight_a = weigh(dot_nt(query_embed, neg_a_ref[...]), positive)
    weight_b = weigh(dot_nt(query_embed, neg_b_ref[...]), positive)
    total = row_sum(weight_a.astype(f32)) + row_sum(weight_b.astype(f32)) + hard
    grad = dot_nn(weight_a, neg_a_ref[...]) + dot_nn(weight_b, neg_b_ref[...]) + hard * second_embed - total * first_embed
    grad = grad - query_unit * row_sum(query_unit * grad)
    power = jnp.exp(jnp.ceil(jnp.log(query_norm) * (1.0 / log_two)) * log_two).astype(bf16).astype(f32)
    inverse = (16.0 / power).astype(bf16).astype(f32)
    out_ref[:, 0:width] = grad * (power / query_norm)
    out_ref[:, width : 2 * width] = query_float
    lanes = lax.broadcasted_iota(jnp.int32, (count, 128), 1)
    scalars = jnp.where(lanes == 0, inverse, 0.0)
    for place, value in ((1, total), (3, hard), (5, first_norm), (7, second_norm), (9, positive)):
        high = value.astype(bf16).astype(f32)
        scalars = jnp.where(lanes == place, high, scalars)
        scalars = jnp.where(lanes == place + 1, value - high, scalars)
    out_ref[:, 2 * width :] = scalars


def node_grad_kernel(own_w_ref, sib_w_ref, own_ref, sib_ref, plane_ref, neg_ref, out_ref, row_ref, neg_w_ref):
    step = pl.program_id(0)
    width = plane_ref.shape[1]
    received = (own_ref, sib_ref)

    @pl.when(step == 0)
    def _():
        for side, ref in enumerate(received):
            scalars = ref[:, 2 * width :].astype(f32).T
            total = scalars[1:2] + scalars[2:3]
            hard = scalars[3:4] + scalars[4:5]
            row_ref[side, 0:1] = scalars[0:1] * 0.0625
            row_ref[side, 1:2] = -total / (scalars[5:6] + scalars[6:7])
            row_ref[side, 2:3] = hard / (scalars[7:8] + scalars[8:9])
            scores = dot_nt(neg_ref[...], ref[:, width : 2 * width])
            neg_w_ref[side] = weigh(scores, scalars[9:10] + scalars[10:11])

    negs = neg_ref.shape[0]
    rows = lax.broadcasted_iota(jnp.int32, (OWN, negs), 0) + step * OWN
    spot = jnp.where(rows == lax.broadcasted_iota(jnp.int32, (OWN, negs), 1) * BLOCK + PART, 1.0, 0.0).astype(bf16)
    hood_part = jnp.zeros((OWN, width), f32)
    query_part = jnp.zeros((OWN, width), f32)
    for side, (w_ref, ref) in enumerate(((own_w_ref, own_ref), (sib_w_ref, sib_ref))):
        w_hood = (w_ref[0].astype(f32) * row_ref[side, 0:1]).astype(bf16)
        hood_part = hood_part + dot_nn(w_hood, ref[:, 0:width])
        w_query = w_ref[1].astype(f32) * row_ref[side, 1:2] + w_ref[2].astype(f32) * row_ref[side, 2:3]
        w_query = (w_query + dot_nn(spot, neg_w_ref[side])).astype(bf16)
        query_part = query_part + dot_nn(w_query, ref[:, width : 2 * width])
    plane = plane_ref[...].astype(f32)
    place = lax.broadcasted_iota(jnp.int32, (OWN, 1), 0) % BLOCK
    inverse = jnp.where(place == PART, 0.0, 1.0 / (row_sum(plane * plane) + epsilon))
    query_part = query_part - plane * (inverse * row_sum(plane * query_part))
    out_ref[...] = (hood_part + query_part).astype(bf16)


def owner_kernel(pieces_ref, pre_ref, out_ref):
    total = pieces_ref[0].astype(f32)
    for k in range(1, pieces_ref.shape[0]):
        total = total + pieces_ref[k].astype(f32)
    pre = pre_ref[...]
    act = pre * jax.nn.sigmoid(pre)
    norm = row_norm(act)
    unit = act / norm
    place = lax.broadcasted_iota(jnp.int32, (BLOCK, 1), 0)
    back = (total - unit * row_sum(unit * total)) / norm
    total = jnp.where(place == PART, back, total)
    out_ref[...] = (total * silu_slope(pre)).astype(bf16)


def table_kernel(neg_row_ref, grad_ref, projection_ref, out_ref):
    out = dot_nt(grad_ref[...], projection_ref[...])
    rows = lax.broadcasted_iota(jnp.int32, (PART, 1), 0)
    for k in range(X):
        block = out[k * BLOCK : k * BLOCK + PART]
        for i in range(X):
            hit = rows + k * PART == neg_row_ref[i]
            block = block + jnp.where(hit, out[i * BLOCK + PART : i * BLOCK + PART + 1], 0.0)
        out_ref[k * PART : (k + 1) * PART] = block


def call(kernel, out_shape, flops, moved, **rest):
    return pl.pallas_call(
        kernel,
        out_shape=out_shape,
        cost_estimate=pl.CostEstimate(flops=flops, bytes_accessed=moved, transcendentals=0),
        compiler_params=pltpu.CompilerParams(vmem_limit_bytes=56 << 20),
        **rest,
    )


VMEM = pl.BlockSpec(memory_space=pltpu.VMEM)
SMEM = pl.BlockSpec(memory_space=pltpu.SMEM)


def on_device(feature_table, projection, slot_owner, slot_row, visits, neg_row):
    z, c, x = (lax.axis_index(a) for a in ("z", "c", "x"))
    here = jnp.stack([z, c]).astype(jnp.int32)
    query_count, slot_count = slot_row.shape
    feat_width, embed_width = projection.shape
    line_count = Z * query_count

    shifted = jnp.pad(visits, ((0, 0), (3, 0)))
    packed = slot_owner.reshape(query_count, slot_count) + slot_row * 128 + shifted * 32768

    rows = jnp.concatenate(
        [
            feature_table.reshape(X, PART, feat_width),
            feature_table[neg_row].reshape(X, 1, feat_width),
            jnp.zeros((X, BLOCK - PART - 1, feat_width), bf16),
        ],
        axis=1,
    ).reshape(OWN, feat_width)
    pre = jnp.dot(rows, projection, preferred_element_type=f32)
    act = jax.nn.silu(pre)
    is_neg = (lax.broadcasted_iota(jnp.int32, (OWN, 1), 0) % BLOCK) == PART
    shared = (act / jnp.where(is_neg, row_norm(act), 1.0)).astype(bf16)
    plane = lax.all_gather(shared, ("y", "c"), axis=0, tiled=True)
    my_pre = lax.dynamic_slice_in_dim(pre, x * BLOCK, BLOCK, axis=0)

    line = lax.all_gather(packed, "z", axis=0, tiled=True)
    spread = call(
        spread_kernel,
        jax.ShapeDtypeStruct((Z, 3, query_count, WIDE), bf16),
        line_count * WIDE * 48,
        line_count * WIDE * 6,
        grid=(Z,),
        in_specs=[SMEM, pl.BlockSpec((query_count, slot_count), lambda i: (i, 0))],
        out_specs=pl.BlockSpec((1, 3, query_count, WIDE), lambda i: (i, 0, 0, 0)),
    )(here, line)
    part = dot_nn(spread.reshape(3 * line_count, WIDE), plane).astype(bf16)
    part, plane, line = lax.optimization_barrier((part, plane, line))
    got = lax.psum_scatter(part, "z", scatter_dimension=0, tiled=True)

    core_plane = lax.dynamic_index_in_dim(plane.reshape(Y, C, X, BLOCK, embed_width), c, axis=1, keepdims=False)
    core_plane = core_plane.transpose(1, 0, 2, 3)
    core_neg = core_plane[:, :, PART].reshape(X * Y, embed_width)
    core_plane = core_plane.reshape(NARROW, embed_width)
    some_neg = lax.all_gather(core_neg, "z", axis=0, tiled=True)
    other_neg = lax.ppermute(some_neg, "c", SIBLING)
    line_sib = lax.ppermute(line, "c", SIBLING)

    def node_weights(some_line):
        return call(
            node_weights_kernel,
            jax.ShapeDtypeStruct((3, NARROW, line_count), bf16),
            line_count * NARROW * 48,
            line_count * NARROW * 6,
            grid=(X,),
            in_specs=[SMEM, pl.BlockSpec((slot_count, line_count), lambda i: (0, 0))],
            out_specs=pl.BlockSpec((3, OWN, line_count), lambda i: (0, i, 0)),
        )(here, some_line.T)

    own_w, sib_w = node_weights(line), node_weights(line_sib)
    got, own_w, sib_w, core_plane, some_neg, other_neg = lax.optimization_barrier(
        (got, own_w, sib_w, core_plane, some_neg, other_neg)
    )

    payload_width = 2 * embed_width + 128
    payload = call(
        query_kernel,
        jax.ShapeDtypeStruct((query_count, payload_width), f32),
        4 * query_count * 512 * embed_width,
        1 << 20,
        in_specs=[VMEM] * 3,
        out_specs=VMEM,
    )(got, some_neg, other_neg)
    own = lax.all_gather(payload.astype(f16), "z", axis=0, tiled=True).astype(bf16)
    sib = lax.ppermute(own, "c", SIBLING)

    node_grads = call(
        node_grad_kernel,
        jax.ShapeDtypeStruct((NARROW, embed_width), bf16),
        8 * line_count * NARROW * embed_width,
        16 << 20,
        grid=(X,),
        in_specs=[
            pl.BlockSpec((3, OWN, line_count), lambda i: (0, i, 0)),
            pl.BlockSpec((3, OWN, line_count), lambda i: (0, i, 0)),
            pl.BlockSpec((line_count, payload_width), lambda i: (0, 0)),
            pl.BlockSpec((line_count, payload_width), lambda i: (0, 0)),
            pl.BlockSpec((OWN, embed_width), lambda i: (i, 0)),
            pl.BlockSpec((X * Y, embed_width), lambda i: (0, 0)),
        ],
        out_specs=pl.BlockSpec((OWN, embed_width), lambda i: (i, 0)),
        scratch_shapes=[pltpu.VMEM((2, 8, line_count), f32), pltpu.VMEM((2, X * Y, line_count), bf16)],
    )(own_w, sib_w, own, sib, core_plane, core_neg)

    pieces = lax.all_to_all(node_grads, ("x", "y"), split_axis=0, concat_axis=0, tiled=True)
    pre_grad = call(
        owner_kernel,
        jax.ShapeDtypeStruct((BLOCK, embed_width), bf16),
        1 << 22,
        3 << 20,
        in_specs=[VMEM] * 2,
        out_specs=VMEM,
    )(pieces.reshape(X * Y, BLOCK, embed_width), my_pre)
    all_pre_grad = lax.all_gather(pre_grad, "x", axis=0, tiled=True)
    return call(
        table_kernel,
        jax.ShapeDtypeStruct((ROWS, feat_width), f32),
        2 * OWN * embed_width * feat_width,
        4 << 20,
        in_specs=[SMEM, VMEM, VMEM],
        out_specs=VMEM,
    )(neg_row, all_pre_grad, projection)


def solution(mesh):
    grid = Mesh(mesh.devices.reshape(Y, Z, C, X), ("y", "z", "c", "x"))
    shard = ("y", "z", "c")
    every = ("y", "z", "c", "x")
    return jax.shard_map(
        on_device,
        mesh=grid,
        in_specs=(
            P(shard, None),
            P(),
            P(every, None, None),
            P(every, None),
            P(every, None),
            P(shard),
        ),
        out_specs=P(shard, None),
        check_vma=False,
    )
```

```python
import jax
import jax.numpy as jnp
from jax import lax
from jax.experimental import pallas as pl
from jax.experimental.pallas import tpu as pltpu
from jax.sharding import Mesh
from jax.sharding import PartitionSpec as P

score_scale = 8.0
margin_value = 0.1
epsilon = 1e-06
log_two = 0.6931471805599453

Y, Z, C, X = 4, 16, 2, 4
ROWS = 256
PART = ROWS // X
BLOCK = PART + 8
OWN = X * BLOCK
WIDE = Y * C * OWN
NARROW = Y * OWN
bf16 = jnp.bfloat16
f16 = jnp.float16
f32 = jnp.float32
SIBLING = [(0, 1), (1, 0)]


def silu_slope(preact):
    gate_value = jax.nn.sigmoid(preact)
    return gate_value * (1.0 + preact * (1.0 - gate_value))


def row_sum(values):
    return jnp.sum(values, axis=1, keepdims=True)


def row_norm(values):
    return jnp.sqrt(row_sum(values * values) + epsilon)


def weigh(score, positive):
    return (score_scale * jax.nn.sigmoid(score_scale * (score - positive + margin_value))).astype(bf16)


def dot_nn(left, right):
    return lax.dot_general(left, right, (((1,), (0,)), ((), ())), preferred_element_type=f32)


def dot_nt(left, right):
    return lax.dot_general(left, right, (((1,), (1,)), ((), ())), preferred_element_type=f32)


def decode(packed, axis):
    owner = packed & 127
    row = (packed >> 7) & 255
    visits = (packed >> 15).astype(f32)
    coefs = visits / jnp.sum(visits, axis=axis, keepdims=True)
    return owner >> 5, owner & 1, (owner >> 1) & 15, row >> 6, row & 63, coefs


def embed_kernel(neg_row_ref, table_ref, projection_ref, pre_ref, shared_ref):
    picks = lax.broadcasted_iota(jnp.int32, (X * 8, ROWS), 0)
    cols = lax.broadcasted_iota(jnp.int32, (X * 8, ROWS), 1)
    hot = jnp.zeros((X * 8, ROWS), f32)
    for i in range(X):
        hot = hot + jnp.where((picks == 8 * i) & (cols == neg_row_ref[i]), 1.0, 0.0)
    neg_rows = dot_nn(hot.astype(bf16), table_ref[...]).astype(bf16)
    neg_pre = dot_nn(neg_rows, projection_ref[...])
    neg_act = neg_pre * jax.nn.sigmoid(neg_pre)
    neg_unit = (neg_act / row_norm(neg_act)).astype(bf16)
    for i in range(X):
        node_pre = dot_nn(table_ref[i * PART : (i + 1) * PART], projection_ref[...])
        start = i * BLOCK
        pre_ref[start : start + PART] = node_pre
        pre_ref[start + PART : start + BLOCK] = neg_pre[8 * i : 8 * i + 8]
        shared_ref[start : start + PART] = (node_pre * jax.nn.sigmoid(node_pre)).astype(bf16)
        shared_ref[start + PART : start + BLOCK] = neg_unit[8 * i : 8 * i + 8]


def spread_kernel(where_ref, line_ref, out_ref):
    ny, nc, nz, part, rest, coefs = decode(line_ref[...], 1)
    column = jnp.where(nz == where_ref[0], (ny * C + nc) * OWN + part * BLOCK + rest, -1)
    rows, slots = column.shape
    chunk = WIDE // 3
    for k in range(3):
        lanes = lax.broadcasted_iota(jnp.int32, (rows, chunk), 1) + k * chunk
        total = jnp.where(lanes == column[:, 0:1], 1.0, 0.0)
        for slot in range(3, slots):
            total = total + jnp.where(lanes == column[:, slot : slot + 1], coefs[:, slot : slot + 1], 0.0)
        span = pl.ds(k * chunk, chunk)
        out_ref[0, 0, :, span] = total.astype(bf16)
        out_ref[0, 1, :, span] = jnp.where(lanes == column[:, 1:2], 1.0, 0.0).astype(bf16)
        out_ref[0, 2, :, span] = jnp.where(lanes == column[:, 2:3], 1.0, 0.0).astype(bf16)


def node_weights_kernel(where_ref, line_ref, out_ref):
    ny, nc, nz, part, rest, coefs = decode(line_ref[...], 0)
    here = (nz == where_ref[0]) & (nc == where_ref[1])
    column = jnp.where(here, part * (Y * BLOCK) + ny * BLOCK + rest, -1)
    slots, count = column.shape
    base = pl.program_id(0) * OWN
    chunk = 32
    for k in range(OWN // chunk):
        nodes = lax.broadcasted_iota(jnp.int32, (chunk, count), 0) + (base + k * chunk)
        total = jnp.where(nodes == column[0:1], 1.0, 0.0)
        for slot in range(3, slots):
            total = total + jnp.where(nodes == column[slot : slot + 1], coefs[slot : slot + 1], 0.0)
        span = pl.ds(k * chunk, chunk)
        out_ref[0, span, :] = total.astype(bf16)
        out_ref[1, span, :] = jnp.where(nodes == column[1:2], 1.0, 0.0).astype(bf16)
        out_ref[2, span, :] = jnp.where(nodes == column[2:3], 1.0, 0.0).astype(bf16)


def query_kernel(got_ref, neg_a_ref, neg_b_ref, out_ref):
    count = got_ref.shape[0] // 3
    width = got_ref.shape[1]
    hood = got_ref[0:count].astype(f32)
    query_norm = row_norm(hood)
    query_unit = hood / query_norm
    query_embed = query_unit.astype(bf16)
    query_float = query_embed.astype(f32)
    first = got_ref[count : 2 * count].astype(f32)
    second = got_ref[2 * count :].astype(f32)
    first_norm, second_norm = row_norm(first), row_norm(second)
    first_embed = (first / first_norm).astype(bf16).astype(f32)
    second_embed = (second / second_norm).astype(bf16).astype(f32)
    positive = row_sum(query_float * first_embed)
    hard = weigh(row_sum(query_float * second_embed), positive).astype(f32)
    weight_a = weigh(dot_nt(query_embed, neg_a_ref[...]), positive)
    weight_b = weigh(dot_nt(query_embed, neg_b_ref[...]), positive)
    total = row_sum(weight_a.astype(f32)) + row_sum(weight_b.astype(f32)) + hard
    grad = dot_nn(weight_a, neg_a_ref[...]) + dot_nn(weight_b, neg_b_ref[...]) + hard * second_embed - total * first_embed
    grad = grad - query_unit * row_sum(query_unit * grad)
    power = jnp.exp(jnp.ceil(jnp.log(query_norm) * (1.0 / log_two)) * log_two).astype(bf16).astype(f32)
    inverse = (16.0 / power).astype(bf16).astype(f32)
    out_ref[:, 0:width] = grad * (power / query_norm)
    out_ref[:, width : 2 * width] = query_float
    lanes = lax.broadcasted_iota(jnp.int32, (count, 128), 1)
    scalars = jnp.where(lanes == 0, inverse, 0.0)
    for place, value in ((1, total), (3, hard), (5, first_norm), (7, second_norm), (9, positive)):
        high = value.astype(bf16).astype(f32)
        scalars = jnp.where(lanes == place, high, scalars)
        scalars = jnp.where(lanes == place + 1, value - high, scalars)
    out_ref[:, 2 * width :] = scalars


def node_grad_kernel(own_w_ref, sib_w_ref, own_ref, sib_ref, plane_ref, neg_ref, out_ref, row_ref, neg_w_ref):
    step = pl.program_id(0)
    width = plane_ref.shape[1]
    received = (own_ref, sib_ref)

    @pl.when(step == 0)
    def _():
        for side, ref in enumerate(received):
            scalars = ref[:, 2 * width :].astype(f32).T
            total = scalars[1:2] + scalars[2:3]
            hard = scalars[3:4] + scalars[4:5]
            row_ref[side, 0:1] = scalars[0:1] * 0.0625
            row_ref[side, 1:2] = -total / (scalars[5:6] + scalars[6:7])
            row_ref[side, 2:3] = hard / (scalars[7:8] + scalars[8:9])
            scores = dot_nt(neg_ref[...], ref[:, width : 2 * width])
            neg_w_ref[side] = weigh(scores, scalars[9:10] + scalars[10:11])

    negs = neg_ref.shape[0]
    rows = lax.broadcasted_iota(jnp.int32, (OWN, negs), 0) + step * OWN
    spot = jnp.where(rows == lax.broadcasted_iota(jnp.int32, (OWN, negs), 1) * BLOCK + PART, 1.0, 0.0).astype(bf16)
    hood_part = jnp.zeros((OWN, width), f32)
    query_part = jnp.zeros((OWN, width), f32)
    for side, (w_ref, ref) in enumerate(((own_w_ref, own_ref), (sib_w_ref, sib_ref))):
        w_hood = (w_ref[0].astype(f32) * row_ref[side, 0:1]).astype(bf16)
        hood_part = hood_part + dot_nn(w_hood, ref[:, 0:width])
        w_query = w_ref[1].astype(f32) * row_ref[side, 1:2] + w_ref[2].astype(f32) * row_ref[side, 2:3]
        w_query = (w_query + dot_nn(spot, neg_w_ref[side])).astype(bf16)
        query_part = query_part + dot_nn(w_query, ref[:, width : 2 * width])
    plane = plane_ref[...].astype(f32)
    place = lax.broadcasted_iota(jnp.int32, (OWN, 1), 0) % BLOCK
    inverse = jnp.where(place == PART, 0.0, 1.0 / (row_sum(plane * plane) + epsilon))
    query_part = query_part - plane * (inverse * row_sum(plane * query_part))
    out_ref[...] = (hood_part + query_part).astype(bf16)


def owner_kernel(pieces_ref, pre_ref, out_ref):
    total = pieces_ref[0].astype(f32)
    for k in range(1, pieces_ref.shape[0]):
        total = total + pieces_ref[k].astype(f32)
    pre = pre_ref[...]
    act = pre * jax.nn.sigmoid(pre)
    norm = row_norm(act)
    unit = act / norm
    place = lax.broadcasted_iota(jnp.int32, (BLOCK, 1), 0)
    back = (total - unit * row_sum(unit * total)) / norm
    total = jnp.where(place == PART, back, total)
    out_ref[...] = (total * silu_slope(pre)).astype(bf16)


def table_kernel(neg_row_ref, grad_ref, projection_ref, out_ref):
    out = dot_nt(grad_ref[...], projection_ref[...])
    rows = lax.broadcasted_iota(jnp.int32, (PART, 1), 0)
    for k in range(X):
        block = out[k * BLOCK : k * BLOCK + PART]
        for i in range(X):
            hit = rows + k * PART == neg_row_ref[i]
            block = block + jnp.where(hit, out[i * BLOCK + PART : i * BLOCK + PART + 1], 0.0)
        out_ref[k * PART : (k + 1) * PART] = block


def call(kernel, out_shape, flops, moved, room, **rest):
    return pl.pallas_call(
        kernel,
        out_shape=out_shape,
        cost_estimate=pl.CostEstimate(flops=flops, bytes_accessed=moved, transcendentals=0),
        compiler_params=pltpu.CompilerParams(vmem_limit_bytes=room << 20),
        **rest,
    )


VMEM = pl.BlockSpec(memory_space=pltpu.VMEM)
SMEM = pl.BlockSpec(memory_space=pltpu.SMEM)


def on_device(feature_table, projection, slot_owner, slot_row, visits, neg_row):
    z, c, x = (lax.axis_index(a) for a in ("z", "c", "x"))
    here = jnp.stack([z, c]).astype(jnp.int32)
    query_count, slot_count = slot_row.shape
    feat_width, embed_width = projection.shape
    line_count = Z * query_count

    shifted = jnp.pad(visits, ((0, 0), (3, 0)))
    packed = slot_owner.reshape(query_count, slot_count) + slot_row * 128 + shifted * 32768

    pre, shared = call(
        embed_kernel,
        (jax.ShapeDtypeStruct((OWN, embed_width), f32), jax.ShapeDtypeStruct((OWN, embed_width), bf16)),
        2 * OWN * embed_width * feat_width,
        5 << 20,
        16,
        in_specs=[SMEM, VMEM, VMEM],
        out_specs=(VMEM, VMEM),
    )(neg_row, feature_table, projection)
    plane = lax.all_gather(shared, ("y", "c"), axis=0, tiled=True)
    my_pre = lax.dynamic_slice_in_dim(pre, x * BLOCK, BLOCK, axis=0)

    copies = jnp.broadcast_to(packed, (Z, query_count, slot_count))
    line = lax.all_to_all(copies, "z", split_axis=0, concat_axis=0, tiled=True).reshape(line_count, slot_count)
    spread = call(
        spread_kernel,
        jax.ShapeDtypeStruct((Z, 3, query_count, WIDE), bf16),
        line_count * WIDE * 48,
        line_count * WIDE * 6,
        16,
        grid=(Z,),
        in_specs=[SMEM, pl.BlockSpec((query_count, slot_count), lambda i: (i, 0))],
        out_specs=pl.BlockSpec((1, 3, query_count, WIDE), lambda i: (i, 0, 0, 0)),
    )(here, line)
    part = dot_nn(spread.reshape(3 * line_count, WIDE), plane).astype(bf16)
    part, plane, line = lax.optimization_barrier((part, plane, line))
    got = lax.psum_scatter(part, "z", scatter_dimension=0, tiled=True)

    core_plane = lax.dynamic_index_in_dim(plane.reshape(Y, C, X, BLOCK, embed_width), c, axis=1, keepdims=False)
    core_plane = core_plane.transpose(1, 0, 2, 3)
    core_neg = core_plane[:, :, PART].reshape(X * Y, embed_width)
    core_plane = core_plane.reshape(NARROW, embed_width)
    some_neg = lax.all_gather(core_neg, "z", axis=0, tiled=True)
    other_neg = lax.ppermute(some_neg, "c", SIBLING)
    line_sib = lax.ppermute(line, "c", SIBLING)

    def node_weights(some_line):
        return call(
            node_weights_kernel,
            jax.ShapeDtypeStruct((3, NARROW, line_count), bf16),
            line_count * NARROW * 48,
            line_count * NARROW * 6,
            12,
            grid=(X,),
            in_specs=[SMEM, pl.BlockSpec((slot_count, line_count), lambda i: (0, 0))],
            out_specs=pl.BlockSpec((3, OWN, line_count), lambda i: (0, i, 0)),
        )(here, some_line.T)

    own_w, sib_w = node_weights(line), node_weights(line_sib)
    got, own_w, sib_w, core_plane, some_neg, other_neg, my_pre = lax.optimization_barrier(
        (got, own_w, sib_w, core_plane, some_neg, other_neg, my_pre)
    )

    payload_width = 2 * embed_width + 128
    payload = call(
        query_kernel,
        jax.ShapeDtypeStruct((query_count, payload_width), f32),
        4 * query_count * 512 * embed_width,
        1 << 20,
        10,
        in_specs=[VMEM] * 3,
        out_specs=VMEM,
    )(got, some_neg, other_neg)
    own = lax.all_gather(payload.astype(f16), "z", axis=0, tiled=True).astype(bf16)
    sib = lax.ppermute(own, "c", SIBLING)

    node_grads = call(
        node_grad_kernel,
        jax.ShapeDtypeStruct((NARROW, embed_width), bf16),
        8 * line_count * NARROW * embed_width,
        16 << 20,
        36,
        grid=(X,),
        in_specs=[
            pl.BlockSpec((3, OWN, line_count), lambda i: (0, i, 0)),
            pl.BlockSpec((3, OWN, line_count), lambda i: (0, i, 0)),
            pl.BlockSpec((line_count, payload_width), lambda i: (0, 0)),
            pl.BlockSpec((line_count, payload_width), lambda i: (0, 0)),
            pl.BlockSpec((OWN, embed_width), lambda i: (i, 0)),
            pl.BlockSpec((X * Y, embed_width), lambda i: (0, 0)),
        ],
        out_specs=pl.BlockSpec((OWN, embed_width), lambda i: (i, 0)),
        scratch_shapes=[pltpu.VMEM((2, 8, line_count), f32), pltpu.VMEM((2, X * Y, line_count), bf16)],
    )(own_w, sib_w, own, sib, core_plane, core_neg)

    pieces = lax.all_to_all(node_grads, ("x", "y"), split_axis=0, concat_axis=0, tiled=True)
    pre_grad = call(
        owner_kernel,
        jax.ShapeDtypeStruct((BLOCK, embed_width), bf16),
        1 << 22,
        3 << 20,
        10,
        in_specs=[VMEM] * 2,
        out_specs=VMEM,
    )(pieces.reshape(X * Y, BLOCK, embed_width), my_pre)
    all_pre_grad = lax.all_gather(pre_grad, "x", axis=0, tiled=True)
    return call(
        table_kernel,
        jax.ShapeDtypeStruct((ROWS, feat_width), f32),
        2 * OWN * embed_width * feat_width,
        4 << 20,
        16,
        in_specs=[SMEM, VMEM, VMEM],
        out_specs=VMEM,
    )(neg_row, all_pre_grad, projection)


def solution(mesh):
    grid = Mesh(mesh.devices.reshape(Y, Z, C, X), ("y", "z", "c", "x"))
    shard = ("y", "z", "c")
    every = ("y", "z", "c", "x")
    return jax.shard_map(
        on_device,
        mesh=grid,
        in_specs=(
            P(shard, None),
            P(),
            P(every, None, None),
            P(every, None),
            P(every, None),
            P(shard),
        ),
        out_specs=P(shard, None),
        check_vma=False,
    )
```

```python
import jax
import jax.numpy as jnp
from jax import lax
from jax.experimental import pallas as pl
from jax.experimental.pallas import tpu as pltpu
from jax.sharding import Mesh
from jax.sharding import PartitionSpec as P

score_scale = 8.0
margin_value = 0.1
epsilon = 1e-06
log_two = 0.6931471805599453

Y, Z, C, X = 4, 16, 2, 4
ROWS = 256
PART = ROWS // X
BLOCK = PART + 8
OWN = X * BLOCK
WIDE = Y * C * OWN
NARROW = Y * OWN
bf16 = jnp.bfloat16
f16 = jnp.float16
f32 = jnp.float32
SIBLING = [(0, 1), (1, 0)]


def silu_slope(preact):
    gate_value = jax.nn.sigmoid(preact)
    return gate_value * (1.0 + preact * (1.0 - gate_value))


def row_sum(values):
    return jnp.sum(values, axis=1, keepdims=True)


def row_norm(values):
    return jnp.sqrt(row_sum(values * values) + epsilon)


def weigh(score, positive):
    return (score_scale * jax.nn.sigmoid(score_scale * (score - positive + margin_value))).astype(bf16)


def dot_nn(left, right):
    return lax.dot_general(left, right, (((1,), (0,)), ((), ())), preferred_element_type=f32)


def dot_nt(left, right):
    return lax.dot_general(left, right, (((1,), (1,)), ((), ())), preferred_element_type=f32)


def decode(packed, axis):
    owner = packed & 127
    row = (packed >> 7) & 255
    visits = (packed >> 15).astype(f32)
    coefs = visits / jnp.sum(visits, axis=axis, keepdims=True)
    return owner >> 5, owner & 1, (owner >> 1) & 15, row >> 6, row & 63, coefs


def embed_kernel(neg_row_ref, table_ref, projection_ref, pre_ref, shared_ref):
    picks = lax.broadcasted_iota(jnp.int32, (X * 8, ROWS), 0)
    cols = lax.broadcasted_iota(jnp.int32, (X * 8, ROWS), 1)
    hot = jnp.zeros((X * 8, ROWS), f32)
    for i in range(X):
        hot = hot + jnp.where((picks == 8 * i) & (cols == neg_row_ref[i]), 1.0, 0.0)
    neg_rows = dot_nn(hot.astype(bf16), table_ref[...]).astype(bf16)
    neg_pre = dot_nn(neg_rows, projection_ref[...])
    neg_act = neg_pre * jax.nn.sigmoid(neg_pre)
    neg_unit = (neg_act / row_norm(neg_act)).astype(bf16)
    for i in range(X):
        node_pre = dot_nn(table_ref[i * PART : (i + 1) * PART], projection_ref[...])
        start = i * BLOCK
        pre_ref[start : start + PART] = node_pre
        pre_ref[start + PART : start + BLOCK] = neg_pre[8 * i : 8 * i + 8]
        shared_ref[start : start + PART] = (node_pre * jax.nn.sigmoid(node_pre)).astype(bf16)
        shared_ref[start + PART : start + BLOCK] = neg_unit[8 * i : 8 * i + 8]


def spread_kernel(where_ref, line_ref, out_ref):
    ny, nc, nz, part, rest, coefs = decode(line_ref[...], 1)
    column = jnp.where(nz == where_ref[0], (ny * C + nc) * OWN + part * BLOCK + rest, -1)
    rows, slots = column.shape
    chunk = WIDE // 3
    for k in range(3):
        lanes = lax.broadcasted_iota(jnp.int32, (rows, chunk), 1) + k * chunk
        total = jnp.where(lanes == column[:, 0:1], 1.0, 0.0)
        for slot in range(3, slots):
            total = total + jnp.where(lanes == column[:, slot : slot + 1], coefs[:, slot : slot + 1], 0.0)
        span = pl.ds(k * chunk, chunk)
        out_ref[0, :, span] = total.astype(bf16)
        out_ref[1, :, span] = jnp.where(lanes == column[:, 1:2], 1.0, 0.0).astype(bf16)
        out_ref[2, :, span] = jnp.where(lanes == column[:, 2:3], 1.0, 0.0).astype(bf16)


def node_weights_kernel(where_ref, line_ref, out_ref):
    ny, nc, nz, part, rest, coefs = decode(line_ref[...], 0)
    here = (nz == where_ref[0]) & (nc == where_ref[1])
    column = jnp.where(here, part * (Y * BLOCK) + ny * BLOCK + rest, -1)
    slots, count = column.shape
    base = pl.program_id(0) * OWN
    chunk = 32
    for k in range(OWN // chunk):
        nodes = lax.broadcasted_iota(jnp.int32, (chunk, count), 0) + (base + k * chunk)
        total = jnp.where(nodes == column[0:1], 1.0, 0.0)
        for slot in range(3, slots):
            total = total + jnp.where(nodes == column[slot : slot + 1], coefs[slot : slot + 1], 0.0)
        span = pl.ds(k * chunk, chunk)
        out_ref[0, span, :] = total.astype(bf16)
        out_ref[1, span, :] = jnp.where(nodes == column[1:2], 1.0, 0.0).astype(bf16)
        out_ref[2, span, :] = jnp.where(nodes == column[2:3], 1.0, 0.0).astype(bf16)


def query_kernel(where_ref, got_ref, neg_a_ref, neg_b_ref, out_ref):
    count, width = got_ref.shape[1:]
    hood = got_ref[0].astype(f32)
    query_norm = row_norm(hood)
    query_unit = hood / query_norm
    query_embed = query_unit.astype(bf16)
    query_float = query_embed.astype(f32)
    first = got_ref[1].astype(f32)
    second = got_ref[2].astype(f32)
    first_norm, second_norm = row_norm(first), row_norm(second)
    first_embed = (first / first_norm).astype(bf16).astype(f32)
    second_embed = (second / second_norm).astype(bf16).astype(f32)
    positive = row_sum(query_float * first_embed)
    hard = weigh(row_sum(query_float * second_embed), positive).astype(f32)
    weight_a = weigh(dot_nt(query_embed, neg_a_ref[...]), positive)
    weight_b = weigh(dot_nt(query_embed, neg_b_ref[...]), positive)
    total = row_sum(weight_a.astype(f32)) + row_sum(weight_b.astype(f32)) + hard
    grad = dot_nn(weight_a, neg_a_ref[...]) + dot_nn(weight_b, neg_b_ref[...]) + hard * second_embed - total * first_embed
    grad = grad - query_unit * row_sum(query_unit * grad)
    power = jnp.exp(jnp.ceil(jnp.log(query_norm) * (1.0 / log_two)) * log_two).astype(bf16).astype(f32)
    inverse = (16.0 / power).astype(bf16).astype(f32)
    out_ref[0:count] = grad * (power / query_norm)
    out_ref[count : 2 * count] = query_float
    lanes = lax.broadcasted_iota(jnp.int32, (count, 128), 1)
    scalars = jnp.where(lanes == 0, inverse, 0.0)
    for place, value in ((1, total), (3, hard), (5, first_norm), (7, second_norm), (9, positive)):
        high = value.astype(bf16).astype(f32)
        scalars = jnp.where(lanes == place, high, scalars)
        scalars = jnp.where(lanes == place + 1, value - high, scalars)
    line_count = Z * count
    spots = lax.broadcasted_iota(jnp.int32, (count, line_count), 0) + where_ref[0] * count
    spots = jnp.where(spots == lax.broadcasted_iota(jnp.int32, (count, line_count), 1), 1.0, 0.0)
    across = dot_nn(scalars.T[0:16].astype(bf16), spots.astype(bf16))
    out_ref[2 * count : 2 * count + 8, 0:line_count] = across[0:8]
    out_ref[2 * count : 2 * count + 8, line_count : 2 * line_count] = across[8:16]


def node_grad_kernel(own_w_ref, sib_w_ref, own_ref, sib_ref, plane_ref, neg_ref, out_ref, row_ref, neg_w_ref):
    step = pl.program_id(0)
    width = plane_ref.shape[1]
    count = (own_ref.shape[1] - 8) // 2
    line_count = Z * count
    received = (own_ref, sib_ref)

    @pl.when(step == 0)
    def _():
        for side, ref in enumerate(received):
            spread = jnp.sum(ref[:, 2 * count : 2 * count + 8].astype(f32), axis=0)
            scalars = jnp.concatenate([spread[:, :line_count], spread[:, line_count:]], axis=0)
            total = scalars[1:2] + scalars[2:3]
            hard = scalars[3:4] + scalars[4:5]
            row_ref[side, 0:1] = scalars[0:1] * 0.0625
            row_ref[side, 1:2] = -total / (scalars[5:6] + scalars[6:7])
            row_ref[side, 2:3] = hard / (scalars[7:8] + scalars[8:9])
            scores = dot_nt(neg_ref[...], ref[:, count : 2 * count].reshape(line_count, width))
            neg_w_ref[side] = weigh(scores, scalars[9:10] + scalars[10:11])

    negs = neg_ref.shape[0]
    rows = lax.broadcasted_iota(jnp.int32, (OWN, negs), 0) + step * OWN
    spot = jnp.where(rows == lax.broadcasted_iota(jnp.int32, (OWN, negs), 1) * BLOCK + PART, 1.0, 0.0).astype(bf16)
    hood_part = jnp.zeros((OWN, width), f32)
    query_part = jnp.zeros((OWN, width), f32)
    for side, (w_ref, ref) in enumerate(((own_w_ref, own_ref), (sib_w_ref, sib_ref))):
        w_hood = (w_ref[0].astype(f32) * row_ref[side, 0:1]).astype(bf16)
        hood_part = hood_part + dot_nn(w_hood, ref[:, 0:count].reshape(line_count, width))
        w_query = w_ref[1].astype(f32) * row_ref[side, 1:2] + w_ref[2].astype(f32) * row_ref[side, 2:3]
        w_query = (w_query + dot_nn(spot, neg_w_ref[side])).astype(bf16)
        query_part = query_part + dot_nn(w_query, ref[:, count : 2 * count].reshape(line_count, width))
    plane = plane_ref[...].astype(f32)
    place = lax.broadcasted_iota(jnp.int32, (OWN, 1), 0) % BLOCK
    inverse = jnp.where(place == PART, 0.0, 1.0 / (row_sum(plane * plane) + epsilon))
    query_part = query_part - plane * (inverse * row_sum(plane * query_part))
    out_ref[...] = (hood_part + query_part).astype(bf16)


def owner_kernel(pieces_ref, pre_ref, out_ref):
    total = pieces_ref[0].astype(f32)
    for k in range(1, pieces_ref.shape[0]):
        total = total + pieces_ref[k].astype(f32)
    pre = pre_ref[...]
    act = pre * jax.nn.sigmoid(pre)
    norm = row_norm(act)
    unit = act / norm
    place = lax.broadcasted_iota(jnp.int32, (BLOCK, 1), 0)
    back = (total - unit * row_sum(unit * total)) / norm
    total = jnp.where(place == PART, back, total)
    out_ref[...] = (total * silu_slope(pre)).astype(bf16)


def table_kernel(neg_row_ref, grad_ref, projection_ref, out_ref):
    out = dot_nt(grad_ref[...], projection_ref[...])
    rows = lax.broadcasted_iota(jnp.int32, (PART, 1), 0)
    for k in range(X):
        block = out[k * BLOCK : k * BLOCK + PART]
        for i in range(X):
            hit = rows + k * PART == neg_row_ref[i]
            block = block + jnp.where(hit, out[i * BLOCK + PART : i * BLOCK + PART + 1], 0.0)
        out_ref[k * PART : (k + 1) * PART] = block


def call(kernel, out_shape, flops, moved, room, **rest):
    return pl.pallas_call(
        kernel,
        out_shape=out_shape,
        cost_estimate=pl.CostEstimate(flops=flops, bytes_accessed=moved, transcendentals=0),
        compiler_params=pltpu.CompilerParams(vmem_limit_bytes=room << 20),
        **rest,
    )


VMEM = pl.BlockSpec(memory_space=pltpu.VMEM)
SMEM = pl.BlockSpec(memory_space=pltpu.SMEM)


def on_device(feature_table, projection, slot_owner, slot_row, visits, neg_row):
    z, c, x = (lax.axis_index(a) for a in ("z", "c", "x"))
    here = jnp.stack([z, c]).astype(jnp.int32)
    query_count, slot_count = slot_row.shape
    feat_width, embed_width = projection.shape
    line_count = Z * query_count

    shifted = jnp.pad(visits, ((0, 0), (3, 0)))
    packed = slot_owner.reshape(query_count, slot_count) + slot_row * 128 + shifted * 32768

    pre, shared = call(
        embed_kernel,
        (jax.ShapeDtypeStruct((OWN, embed_width), f32), jax.ShapeDtypeStruct((OWN, embed_width), bf16)),
        2 * OWN * embed_width * feat_width,
        5 << 20,
        16,
        in_specs=[SMEM, VMEM, VMEM],
        out_specs=(VMEM, VMEM),
    )(neg_row, feature_table, projection)
    plane = lax.all_gather(shared, ("y", "c"), axis=0, tiled=True)
    my_pre = lax.dynamic_slice_in_dim(pre, x * BLOCK, BLOCK, axis=0)

    copies = jnp.broadcast_to(packed, (Z, query_count, slot_count))
    line = lax.all_to_all(copies, "z", split_axis=0, concat_axis=0, tiled=True).reshape(line_count, slot_count)
    spread = call(
        spread_kernel,
        jax.ShapeDtypeStruct((3, line_count, WIDE), bf16),
        line_count * WIDE * 48,
        line_count * WIDE * 6,
        16,
        grid=(Z,),
        in_specs=[SMEM, pl.BlockSpec((query_count, slot_count), lambda i: (i, 0))],
        out_specs=pl.BlockSpec((3, query_count, WIDE), lambda i: (0, i, 0)),
    )(here, line)
    part = dot_nn(spread.reshape(3 * line_count, WIDE), plane).astype(bf16)
    part, plane, line = lax.optimization_barrier((part, plane, line))
    got = lax.psum_scatter(
        part.reshape(3, line_count, embed_width), "z", scatter_dimension=1, tiled=True
    )

    core_plane = lax.dynamic_index_in_dim(plane.reshape(Y, C, X, BLOCK, embed_width), c, axis=1, keepdims=False)
    core_plane = core_plane.transpose(1, 0, 2, 3)
    core_neg = core_plane[:, :, PART].reshape(X * Y, embed_width)
    core_plane = core_plane.reshape(NARROW, embed_width)
    some_neg = lax.all_gather(core_neg, "z", axis=0, tiled=True)
    other_neg = lax.ppermute(some_neg, "c", SIBLING)
    line_sib = lax.ppermute(line, "c", SIBLING)

    def node_weights(some_line):
        return call(
            node_weights_kernel,
            jax.ShapeDtypeStruct((3, NARROW, line_count), bf16),
            line_count * NARROW * 48,
            line_count * NARROW * 6,
            12,
            grid=(X,),
            in_specs=[SMEM, pl.BlockSpec((slot_count, line_count), lambda i: (0, 0))],
            out_specs=pl.BlockSpec((3, OWN, line_count), lambda i: (0, i, 0)),
        )(here, some_line.T)

    own_w, sib_w = node_weights(line), node_weights(line_sib)
    got, own_w, sib_w, core_plane, some_neg, other_neg, my_pre = lax.optimization_barrier(
        (got, own_w, sib_w, core_plane, some_neg, other_neg, my_pre)
    )

    payload_rows = 2 * query_count + 8
    payload = call(
        query_kernel,
        jax.ShapeDtypeStruct((payload_rows, embed_width), f32),
        4 * query_count * 512 * embed_width,
        1 << 20,
        10,
        in_specs=[SMEM] + [VMEM] * 3,
        out_specs=VMEM,
    )(here, got, some_neg, other_neg)
    own = lax.all_gather(payload.astype(f16), "z", axis=0, tiled=True).astype(bf16)
    own = own.reshape(Z, payload_rows, embed_width)
    sib = lax.ppermute(own, "c", SIBLING)

    node_grads = call(
        node_grad_kernel,
        jax.ShapeDtypeStruct((NARROW, embed_width), bf16),
        8 * line_count * NARROW * embed_width,
        16 << 20,
        36,
        grid=(X,),
        in_specs=[
            pl.BlockSpec((3, OWN, line_count), lambda i: (0, i, 0)),
            pl.BlockSpec((3, OWN, line_count), lambda i: (0, i, 0)),
            pl.BlockSpec((Z, payload_rows, embed_width), lambda i: (0, 0, 0)),
            pl.BlockSpec((Z, payload_rows, embed_width), lambda i: (0, 0, 0)),
            pl.BlockSpec((OWN, embed_width), lambda i: (i, 0)),
            pl.BlockSpec((X * Y, embed_width), lambda i: (0, 0)),
        ],
        out_specs=pl.BlockSpec((OWN, embed_width), lambda i: (i, 0)),
        scratch_shapes=[pltpu.VMEM((2, 8, line_count), f32), pltpu.VMEM((2, X * Y, line_count), bf16)],
    )(own_w, sib_w, own, sib, core_plane, core_neg)

    pieces = lax.all_to_all(node_grads, ("x", "y"), split_axis=0, concat_axis=0, tiled=True)
    pre_grad = call(
        owner_kernel,
        jax.ShapeDtypeStruct((BLOCK, embed_width), bf16),
        1 << 22,
        3 << 20,
        10,
        in_specs=[VMEM] * 2,
        out_specs=VMEM,
    )(pieces.reshape(X * Y, BLOCK, embed_width), my_pre)
    all_pre_grad = lax.all_gather(pre_grad, "x", axis=0, tiled=True)
    return call(
        table_kernel,
        jax.ShapeDtypeStruct((ROWS, feat_width), f32),
        2 * OWN * embed_width * feat_width,
        4 << 20,
        16,
        in_specs=[SMEM, VMEM, VMEM],
        out_specs=VMEM,
    )(neg_row, all_pre_grad, projection)


def solution(mesh):
    grid = Mesh(mesh.devices.reshape(Y, Z, C, X), ("y", "z", "c", "x"))
    shard = ("y", "z", "c")
    every = ("y", "z", "c", "x")
    return jax.shard_map(
        on_device,
        mesh=grid,
        in_specs=(
            P(shard, None),
            P(),
            P(every, None, None),
            P(every, None),
            P(every, None),
            P(shard),
        ),
        out_specs=P(shard, None),
        check_vma=False,
    )
```

```python
import jax
import jax.numpy as jnp
from jax import lax
from jax.experimental import pallas as pl
from jax.experimental.pallas import tpu as pltpu
from jax.sharding import Mesh
from jax.sharding import PartitionSpec as P

score_scale = 8.0
margin_value = 0.1
epsilon = 1e-06
log_two = 0.6931471805599453

Y, Z, C, X = 4, 16, 2, 4
ROWS = 256
PART = ROWS // X
BLOCK = PART + 8
OWN = X * BLOCK
WIDE = Y * C * OWN
NARROW = Y * OWN
bf16 = jnp.bfloat16
f16 = jnp.float16
f32 = jnp.float32
SIBLING = [(0, 1), (1, 0)]


def silu_slope(preact):
    gate_value = jax.nn.sigmoid(preact)
    return gate_value * (1.0 + preact * (1.0 - gate_value))


def row_sum(values):
    return jnp.sum(values, axis=1, keepdims=True)


def row_norm(values):
    return jnp.sqrt(row_sum(values * values) + epsilon)


def weigh(score, positive):
    return (score_scale * jax.nn.sigmoid(score_scale * (score - positive + margin_value))).astype(bf16)


def dot_nn(left, right):
    return lax.dot_general(left, right, (((1,), (0,)), ((), ())), preferred_element_type=f32)


def dot_nt(left, right):
    return lax.dot_general(left, right, (((1,), (1,)), ((), ())), preferred_element_type=f32)


def decode(packed, axis):
    owner = packed & 127
    row = (packed >> 7) & 255
    visits = (packed >> 15).astype(f32)
    coefs = visits / jnp.sum(visits, axis=axis, keepdims=True)
    return owner >> 5, owner & 1, (owner >> 1) & 15, row >> 6, row & 63, coefs


def embed_kernel(neg_row_ref, table_ref, projection_ref, pre_ref, shared_ref, negs_ref):
    picks = lax.broadcasted_iota(jnp.int32, (X * 8, ROWS), 0)
    cols = lax.broadcasted_iota(jnp.int32, (X * 8, ROWS), 1)
    hot = jnp.zeros((X * 8, ROWS), f32)
    for i in range(X):
        hot = hot + jnp.where((picks == 8 * i) & (cols == neg_row_ref[i]), 1.0, 0.0)
    neg_rows = dot_nn(hot.astype(bf16), table_ref[...]).astype(bf16)
    neg_pre = dot_nn(neg_rows, projection_ref[...])
    neg_act = neg_pre * jax.nn.sigmoid(neg_pre)
    neg_unit = (neg_act / row_norm(neg_act)).astype(bf16)
    source = lax.broadcasted_iota(jnp.int32, (8, X * 8), 0) * 8
    pick = jnp.where(source == lax.broadcasted_iota(jnp.int32, (8, X * 8), 1), 1.0, 0.0)
    negs_ref[...] = dot_nn(pick.astype(bf16), neg_unit).astype(bf16)
    for i in range(X):
        node_pre = dot_nn(table_ref[i * PART : (i + 1) * PART], projection_ref[...])
        start = i * BLOCK
        pre_ref[start : start + PART] = node_pre
        pre_ref[start + PART : start + BLOCK] = neg_pre[8 * i : 8 * i + 8]
        shared_ref[start : start + PART] = (node_pre * jax.nn.sigmoid(node_pre)).astype(bf16)
        shared_ref[start + PART : start + BLOCK] = neg_unit[8 * i : 8 * i + 8]


def spread_kernel(where_ref, received_ref, out_ref, line_ref):
    rows, slots = line_ref.shape
    tiles = [received_ref[0, X:8, t * 128 : (t + 1) * 128].astype(f32) for t in range(8)]
    fields = jnp.concatenate(tiles, axis=0)
    packed = fields[:, 0:slots] + fields[:, slots : 2 * slots] * 128.0 + fields[:, 2 * slots : 3 * slots] * 32768.0
    packed = packed.astype(jnp.int32)
    line_ref[...] = packed
    ny, nc, nz, part, rest, coefs = decode(packed, 1)
    column = jnp.where(nz == where_ref[0], (ny * C + nc) * OWN + part * BLOCK + rest, -1)
    high, low = column >> 8, column & 255
    lanes = lax.broadcasted_iota(jnp.int32, (rows, 256), 1)
    chunks = WIDE // 256
    totals = [jnp.zeros((rows, 256), bf16) for _ in range(chunks)]
    for slot in range(slots):
        hot = jnp.where(lanes == low[:, slot : slot + 1], 1.0, 0.0).astype(bf16)
        weight = coefs[:, slot : slot + 1] if slot > 2 else 1.0
        for k in range(chunks):
            term = hot * jnp.where(high[:, slot : slot + 1] == k, weight, 0.0).astype(bf16)
            if slot == 1 or slot == 2:
                out_ref[slot, :, k * 256 : (k + 1) * 256] = term
            else:
                totals[k] = totals[k] + term
    for k in range(chunks):
        out_ref[0, :, k * 256 : (k + 1) * 256] = totals[k]


def node_weights_kernel(where_ref, line_ref, out_ref):
    ny, nc, nz, part, rest, coefs = decode(line_ref[...], 0)
    here = (nz == where_ref[0]) & (nc == where_ref[1])
    column = jnp.where(here, part * (Y * BLOCK) + ny * BLOCK + rest, -1)
    slots, count = column.shape
    base = pl.program_id(0) * OWN
    chunk = 32
    for k in range(OWN // chunk):
        nodes = lax.broadcasted_iota(jnp.int32, (chunk, count), 0) + (base + k * chunk)
        total = jnp.where(nodes == column[0:1], 1.0, 0.0)
        for slot in range(3, slots):
            total = total + jnp.where(nodes == column[slot : slot + 1], coefs[slot : slot + 1], 0.0)
        span = pl.ds(k * chunk, chunk)
        out_ref[0, span, :] = total.astype(bf16)
        out_ref[1, span, :] = jnp.where(nodes == column[1:2], 1.0, 0.0).astype(bf16)
        out_ref[2, span, :] = jnp.where(nodes == column[2:3], 1.0, 0.0).astype(bf16)


def query_kernel(where_ref, got_ref, neg_a_ref, neg_b_ref, out_ref):
    count, width = got_ref.shape[1:]
    hood = got_ref[0].astype(f32)
    query_norm = row_norm(hood)
    query_unit = hood / query_norm
    query_embed = query_unit.astype(bf16)
    query_float = query_embed.astype(f32)
    first = got_ref[1].astype(f32)
    second = got_ref[2].astype(f32)
    first_norm, second_norm = row_norm(first), row_norm(second)
    first_embed = (first / first_norm).astype(bf16).astype(f32)
    second_embed = (second / second_norm).astype(bf16).astype(f32)
    positive = row_sum(query_float * first_embed)
    hard = weigh(row_sum(query_float * second_embed), positive).astype(f32)
    weight_a = weigh(dot_nt(query_embed, neg_a_ref[...]), positive)
    weight_b = weigh(dot_nt(query_embed, neg_b_ref[...]), positive)
    total = row_sum(weight_a.astype(f32)) + row_sum(weight_b.astype(f32)) + hard
    grad = dot_nn(weight_a, neg_a_ref[...]) + dot_nn(weight_b, neg_b_ref[...]) + hard * second_embed - total * first_embed
    grad = grad - query_unit * row_sum(query_unit * grad)
    power = jnp.exp(jnp.ceil(jnp.log(query_norm) * (1.0 / log_two)) * log_two).astype(bf16).astype(f32)
    inverse = (16.0 / power).astype(bf16).astype(f32)
    out_ref[0:count] = grad * (power / query_norm)
    out_ref[count : 2 * count] = query_float
    lanes = lax.broadcasted_iota(jnp.int32, (count, 128), 1)
    scalars = jnp.where(lanes == 0, inverse, 0.0)
    for place, value in ((1, total), (3, hard), (5, first_norm), (7, second_norm), (9, positive)):
        high = value.astype(bf16).astype(f32)
        scalars = jnp.where(lanes == place, high, scalars)
        scalars = jnp.where(lanes == place + 1, value - high, scalars)
    line_count = Z * count
    spots = lax.broadcasted_iota(jnp.int32, (count, line_count), 0) + where_ref[0] * count
    spots = jnp.where(spots == lax.broadcasted_iota(jnp.int32, (count, line_count), 1), 1.0, 0.0)
    across = dot_nn(scalars.T[0:16].astype(bf16), spots.astype(bf16))
    out_ref[2 * count : 2 * count + 8, 0:line_count] = across[0:8]
    out_ref[2 * count : 2 * count + 8, line_count : 2 * line_count] = across[8:16]


def node_grad_kernel(own_w_ref, sib_w_ref, own_ref, sib_ref, plane_ref, neg_ref, out_ref, row_ref, neg_w_ref):
    step = pl.program_id(0)
    width = plane_ref.shape[1]
    count = (own_ref.shape[1] - 8) // 2
    line_count = Z * count
    received = (own_ref, sib_ref)

    @pl.when(step == 0)
    def _():
        for side, ref in enumerate(received):
            spread = jnp.sum(ref[:, 2 * count : 2 * count + 8].astype(f32), axis=0)
            scalars = jnp.concatenate([spread[:, :line_count], spread[:, line_count:]], axis=0)
            total = scalars[1:2] + scalars[2:3]
            hard = scalars[3:4] + scalars[4:5]
            row_ref[side, 0:1] = scalars[0:1] * 0.0625
            row_ref[side, 1:2] = -total / (scalars[5:6] + scalars[6:7])
            row_ref[side, 2:3] = hard / (scalars[7:8] + scalars[8:9])
            scores = dot_nt(neg_ref[...], ref[:, count : 2 * count].reshape(line_count, width))
            neg_w_ref[side] = weigh(scores, scalars[9:10] + scalars[10:11])

    negs = neg_ref.shape[0]
    rows = lax.broadcasted_iota(jnp.int32, (OWN, negs), 0) + step * OWN
    spot = jnp.where(rows == lax.broadcasted_iota(jnp.int32, (OWN, negs), 1) * BLOCK + PART, 1.0, 0.0).astype(bf16)
    hood_part = jnp.zeros((OWN, width), f32)
    query_part = jnp.zeros((OWN, width), f32)
    for side, (w_ref, ref) in enumerate(((own_w_ref, own_ref), (sib_w_ref, sib_ref))):
        w_hood = (w_ref[0].astype(f32) * row_ref[side, 0:1]).astype(bf16)
        hood_part = hood_part + dot_nn(w_hood, ref[:, 0:count].reshape(line_count, width))
        w_query = w_ref[1].astype(f32) * row_ref[side, 1:2] + w_ref[2].astype(f32) * row_ref[side, 2:3]
        w_query = (w_query + dot_nn(spot, neg_w_ref[side])).astype(bf16)
        query_part = query_part + dot_nn(w_query, ref[:, count : 2 * count].reshape(line_count, width))
    plane = plane_ref[...].astype(f32)
    place = lax.broadcasted_iota(jnp.int32, (OWN, 1), 0) % BLOCK
    inverse = jnp.where(place == PART, 0.0, 1.0 / (row_sum(plane * plane) + epsilon))
    query_part = query_part - plane * (inverse * row_sum(plane * query_part))
    out_ref[...] = (hood_part + query_part).astype(bf16)


def owner_kernel(pieces_ref, pre_ref, out_ref):
    total = pieces_ref[0].astype(f32)
    for k in range(1, pieces_ref.shape[0]):
        total = total + pieces_ref[k].astype(f32)
    pre = pre_ref[...]
    act = pre * jax.nn.sigmoid(pre)
    norm = row_norm(act)
    unit = act / norm
    place = lax.broadcasted_iota(jnp.int32, (BLOCK, 1), 0)
    back = (total - unit * row_sum(unit * total)) / norm
    total = jnp.where(place == PART, back, total)
    out_ref[...] = (total * silu_slope(pre)).astype(bf16)


def table_kernel(neg_row_ref, grad_ref, projection_ref, out_ref):
    out = dot_nt(grad_ref[...], projection_ref[...])
    rows = lax.broadcasted_iota(jnp.int32, (PART, 1), 0)
    for k in range(X):
        block = out[k * BLOCK : k * BLOCK + PART]
        for i in range(X):
            hit = rows + k * PART == neg_row_ref[i]
            block = block + jnp.where(hit, out[i * BLOCK + PART : i * BLOCK + PART + 1], 0.0)
        out_ref[k * PART : (k + 1) * PART] = block


def call(kernel, out_shape, flops, moved, room, **rest):
    return pl.pallas_call(
        kernel,
        out_shape=out_shape,
        cost_estimate=pl.CostEstimate(flops=flops, bytes_accessed=moved, transcendentals=0),
        compiler_params=pltpu.CompilerParams(vmem_limit_bytes=room << 20),
        **rest,
    )


VMEM = pl.BlockSpec(memory_space=pltpu.VMEM)
SMEM = pl.BlockSpec(memory_space=pltpu.SMEM)


def on_device(feature_table, projection, slot_owner, slot_row, visits, neg_row):
    z, c, x = (lax.axis_index(a) for a in ("z", "c", "x"))
    here = jnp.stack([z, c]).astype(jnp.int32)
    query_count, slot_count = slot_row.shape
    feat_width, embed_width = projection.shape
    line_count = Z * query_count

    pre, shared, negs = call(
        embed_kernel,
        (
            jax.ShapeDtypeStruct((OWN, embed_width), f32),
            jax.ShapeDtypeStruct((OWN, embed_width), bf16),
            jax.ShapeDtypeStruct((8, embed_width), bf16),
        ),
        2 * OWN * embed_width * feat_width,
        5 << 20,
        16,
        in_specs=[SMEM, VMEM, VMEM],
        out_specs=(VMEM, VMEM, VMEM),
    )(neg_row, feature_table, projection)
    plane = lax.all_gather(shared, ("y", "c"), axis=0, tiled=True)
    my_pre = lax.dynamic_slice_in_dim(pre, x * BLOCK, BLOCK, axis=0)

    shifted = jnp.pad(visits, ((0, 0), (3, 0)))
    fields = jnp.concatenate([slot_owner.reshape(query_count, slot_count), slot_row, shifted], axis=1)
    fields = jnp.pad(fields.astype(bf16), ((0, 0), (0, 128 - 3 * slot_count)))
    fields = fields.reshape(8, 4, 128).transpose(1, 0, 2).reshape(4, embed_width)
    block = jnp.concatenate([negs[0:X], fields], axis=0)
    copies = jnp.broadcast_to(block, (Z, 8, embed_width))
    received = lax.all_to_all(copies, "z", split_axis=0, concat_axis=0, tiled=True)
    line_neg = received[:, 0:X].reshape(Z * X, embed_width)
    spread, line = call(
        spread_kernel,
        (
            jax.ShapeDtypeStruct((3, line_count, WIDE), bf16),
            jax.ShapeDtypeStruct((line_count, slot_count), jnp.int32),
        ),
        line_count * WIDE * 48,
        line_count * WIDE * 6,
        56,
        grid=(Z,),
        in_specs=[SMEM, pl.BlockSpec((1, 8, embed_width), lambda i: (i, 0, 0))],
        out_specs=(
            pl.BlockSpec((3, query_count, WIDE), lambda i: (0, i, 0)),
            pl.BlockSpec((query_count, slot_count), lambda i: (i, 0)),
        ),
    )(here, received)
    part = dot_nn(spread.reshape(3 * line_count, WIDE), plane).astype(bf16)
    part, plane, line, line_neg = lax.optimization_barrier((part, plane, line, line_neg))
    got = lax.psum_scatter(
        part.reshape(3, line_count, embed_width), "z", scatter_dimension=1, tiled=True
    )

    core_plane = lax.dynamic_index_in_dim(plane.reshape(Y, C, X, BLOCK, embed_width), c, axis=1, keepdims=False)
    core_plane = core_plane.transpose(1, 0, 2, 3)
    core_neg = core_plane[:, :, PART].reshape(X * Y, embed_width)
    core_plane = core_plane.reshape(NARROW, embed_width)
    some_neg = lax.all_gather(line_neg, "y", axis=0, tiled=True)
    other_neg = lax.ppermute(some_neg, "c", SIBLING)
    line_sib = lax.ppermute(line, "c", SIBLING)

    def node_weights(some_line):
        return call(
            node_weights_kernel,
            jax.ShapeDtypeStruct((3, NARROW, line_count), bf16),
            line_count * NARROW * 48,
            line_count * NARROW * 6,
            12,
            grid=(X,),
            in_specs=[SMEM, pl.BlockSpec((slot_count, line_count), lambda i: (0, 0))],
            out_specs=pl.BlockSpec((3, OWN, line_count), lambda i: (0, i, 0)),
        )(here, some_line.T)

    own_w, sib_w = node_weights(line), node_weights(line_sib)
    got, own_w, sib_w, core_plane, some_neg, other_neg, my_pre = lax.optimization_barrier(
        (got, own_w, sib_w, core_plane, some_neg, other_neg, my_pre)
    )

    payload_rows = 2 * query_count + 8
    payload = call(
        query_kernel,
        jax.ShapeDtypeStruct((payload_rows, embed_width), f32),
        4 * query_count * 512 * embed_width,
        1 << 20,
        10,
        in_specs=[SMEM] + [VMEM] * 3,
        out_specs=VMEM,
    )(here, got, some_neg, other_neg)
    own = lax.all_gather(payload.astype(f16), "z", axis=0, tiled=True).astype(bf16)
    own = own.reshape(Z, payload_rows, embed_width)
    sib = lax.ppermute(own, "c", SIBLING)

    node_grads = call(
        node_grad_kernel,
        jax.ShapeDtypeStruct((NARROW, embed_width), bf16),
        8 * line_count * NARROW * embed_width,
        16 << 20,
        36,
        grid=(X,),
        in_specs=[
            pl.BlockSpec((3, OWN, line_count), lambda i: (0, i, 0)),
            pl.BlockSpec((3, OWN, line_count), lambda i: (0, i, 0)),
            pl.BlockSpec((Z, payload_rows, embed_width), lambda i: (0, 0, 0)),
            pl.BlockSpec((Z, payload_rows, embed_width), lambda i: (0, 0, 0)),
            pl.BlockSpec((OWN, embed_width), lambda i: (i, 0)),
            pl.BlockSpec((X * Y, embed_width), lambda i: (0, 0)),
        ],
        out_specs=pl.BlockSpec((OWN, embed_width), lambda i: (i, 0)),
        scratch_shapes=[pltpu.VMEM((2, 8, line_count), f32), pltpu.VMEM((2, X * Y, line_count), bf16)],
    )(own_w, sib_w, own, sib, core_plane, core_neg)

    pieces = lax.all_to_all(node_grads, ("x", "y"), split_axis=0, concat_axis=0, tiled=True)
    pre_grad = call(
        owner_kernel,
        jax.ShapeDtypeStruct((BLOCK, embed_width), bf16),
        1 << 22,
        3 << 20,
        10,
        in_specs=[VMEM] * 2,
        out_specs=VMEM,
    )(pieces.reshape(X * Y, BLOCK, embed_width), my_pre)
    all_pre_grad = lax.all_gather(pre_grad, "x", axis=0, tiled=True)
    return call(
        table_kernel,
        jax.ShapeDtypeStruct((ROWS, feat_width), f32),
        2 * OWN * embed_width * feat_width,
        4 << 20,
        16,
        in_specs=[SMEM, VMEM, VMEM],
        out_specs=VMEM,
    )(neg_row, all_pre_grad, projection)


def solution(mesh):
    grid = Mesh(mesh.devices.reshape(Y, Z, C, X), ("y", "z", "c", "x"))
    shard = ("y", "z", "c")
    every = ("y", "z", "c", "x")
    return jax.shard_map(
        on_device,
        mesh=grid,
        in_specs=(
            P(shard, None),
            P(),
            P(every, None, None),
            P(every, None),
            P(every, None),
            P(shard),
        ),
        out_specs=P(shard, None),
        check_vma=False,
    )
```

```python
import jax
import jax.numpy as jnp
from jax import lax
from jax.experimental import pallas as pl
from jax.experimental.pallas import tpu as pltpu
from jax.sharding import Mesh
from jax.sharding import PartitionSpec as P

score_scale = 8.0
margin_value = 0.1
epsilon = 1e-06
log_two = 0.6931471805599453

Y, Z, C, X = 4, 16, 2, 4
ROWS = 256
PART = ROWS // X
BLOCK = PART + 8
OWN = X * BLOCK
WIDE = Y * C * OWN
NARROW = Y * OWN
bf16 = jnp.bfloat16
f16 = jnp.float16
f32 = jnp.float32
SIBLING = [(0, 1), (1, 0)]


def silu_slope(preact):
    gate_value = jax.nn.sigmoid(preact)
    return gate_value * (1.0 + preact * (1.0 - gate_value))


def row_sum(values):
    return jnp.sum(values, axis=1, keepdims=True)


def row_norm(values):
    return jnp.sqrt(row_sum(values * values) + epsilon)


def weigh(score, positive):
    return (score_scale * jax.nn.sigmoid(score_scale * (score - positive + margin_value))).astype(bf16)


def dot_nn(left, right):
    return lax.dot_general(left, right, (((1,), (0,)), ((), ())), preferred_element_type=f32)


def dot_nt(left, right):
    return lax.dot_general(left, right, (((1,), (1,)), ((), ())), preferred_element_type=f32)


def decode(packed, axis):
    owner = packed & 127
    row = (packed >> 7) & 255
    visits = (packed >> 15).astype(f32)
    coefs = visits / jnp.sum(visits, axis=axis, keepdims=True)
    return owner >> 5, owner & 1, (owner >> 1) & 15, row >> 6, row & 63, coefs


def embed_kernel(neg_row_ref, table_ref, projection_ref, pre_ref, shared_ref, negs_ref):
    picks = lax.broadcasted_iota(jnp.int32, (X * 8, ROWS), 0)
    cols = lax.broadcasted_iota(jnp.int32, (X * 8, ROWS), 1)
    hot = jnp.zeros((X * 8, ROWS), f32)
    for i in range(X):
        hot = hot + jnp.where((picks == 8 * i) & (cols == neg_row_ref[i]), 1.0, 0.0)
    neg_rows = dot_nn(hot.astype(bf16), table_ref[...]).astype(bf16)
    neg_pre = dot_nn(neg_rows, projection_ref[...])
    neg_act = neg_pre * jax.nn.sigmoid(neg_pre)
    neg_unit = (neg_act / row_norm(neg_act)).astype(bf16)
    source = lax.broadcasted_iota(jnp.int32, (8, X * 8), 0) * 8
    pick = jnp.where(source == lax.broadcasted_iota(jnp.int32, (8, X * 8), 1), 1.0, 0.0)
    negs_ref[...] = dot_nn(pick.astype(bf16), neg_unit).astype(bf16)
    for i in range(X):
        node_pre = dot_nn(table_ref[i * PART : (i + 1) * PART], projection_ref[...])
        start = i * BLOCK
        pre_ref[start : start + PART] = node_pre
        pre_ref[start + PART : start + BLOCK] = neg_pre[8 * i : 8 * i + 8]
        shared_ref[start : start + PART] = (node_pre * jax.nn.sigmoid(node_pre)).astype(bf16)
        shared_ref[start + PART : start + BLOCK] = neg_unit[8 * i : 8 * i + 8]


def spread_kernel(where_ref, received_ref, out_ref, line_ref):
    rows, slots = line_ref.shape
    tiles = [received_ref[0, X:8, t * 128 : (t + 1) * 128].astype(f32) for t in range(8)]
    fields = jnp.concatenate(tiles, axis=0)
    packed = fields[:, 0:slots] + fields[:, slots : 2 * slots] * 128.0 + fields[:, 2 * slots : 3 * slots] * 32768.0
    packed = packed.astype(jnp.int32)
    line_ref[...] = packed
    ny, nc, nz, part, rest, coefs = decode(packed, 1)
    column = jnp.where(nz == where_ref[0], (ny * C + nc) * OWN + part * BLOCK + rest, -1)
    high, low = column >> 8, column & 255
    lanes = lax.broadcasted_iota(jnp.int32, (rows, 256), 1)
    chunks = WIDE // 256
    totals = [jnp.zeros((rows, 256), bf16) for _ in range(chunks)]
    nothing = jnp.zeros((rows, 256), bf16)
    for slot in range(slots):
        weight = coefs[:, slot : slot + 1] if slot > 2 else 1.0
        hot = jnp.where(lanes == low[:, slot : slot + 1], weight, 0.0).astype(bf16)
        level = jnp.broadcast_to(high[:, slot : slot + 1].astype(f32), (rows, 256)).astype(bf16)
        for k in range(chunks):
            term = jnp.where(level == k, hot, nothing)
            if slot == 1 or slot == 2:
                out_ref[slot, :, k * 256 : (k + 1) * 256] = term
            else:
                totals[k] = totals[k] + term
    for k in range(chunks):
        out_ref[0, :, k * 256 : (k + 1) * 256] = totals[k]


def node_weights_kernel(where_ref, line_ref, out_ref):
    ny, nc, nz, part, rest, coefs = decode(line_ref[...], 0)
    here = (nz == where_ref[0]) & (nc == where_ref[1])
    column = jnp.where(here, part * (Y * BLOCK) + ny * BLOCK + rest, -1)
    slots, count = column.shape
    base = pl.program_id(0) * OWN
    chunk = 32
    for k in range(OWN // chunk):
        nodes = lax.broadcasted_iota(jnp.int32, (chunk, count), 0) + (base + k * chunk)
        total = jnp.where(nodes == column[0:1], 1.0, 0.0)
        for slot in range(3, slots):
            total = total + jnp.where(nodes == column[slot : slot + 1], coefs[slot : slot + 1], 0.0)
        span = pl.ds(k * chunk, chunk)
        out_ref[0, span, :] = total.astype(bf16)
        out_ref[1, span, :] = jnp.where(nodes == column[1:2], 1.0, 0.0).astype(bf16)
        out_ref[2, span, :] = jnp.where(nodes == column[2:3], 1.0, 0.0).astype(bf16)


def query_kernel(where_ref, got_ref, neg_a_ref, neg_b_ref, out_ref):
    count, width = got_ref.shape[1:]
    hood = got_ref[0].astype(f32)
    query_norm = row_norm(hood)
    query_unit = hood / query_norm
    query_embed = query_unit.astype(bf16)
    query_float = query_embed.astype(f32)
    first = got_ref[1].astype(f32)
    second = got_ref[2].astype(f32)
    first_norm, second_norm = row_norm(first), row_norm(second)
    first_embed = (first / first_norm).astype(bf16).astype(f32)
    second_embed = (second / second_norm).astype(bf16).astype(f32)
    positive = row_sum(query_float * first_embed)
    hard = weigh(row_sum(query_float * second_embed), positive).astype(f32)
    weight_a = weigh(dot_nt(query_embed, neg_a_ref[...]), positive)
    weight_b = weigh(dot_nt(query_embed, neg_b_ref[...]), positive)
    total = row_sum(weight_a.astype(f32)) + row_sum(weight_b.astype(f32)) + hard
    grad = dot_nn(weight_a, neg_a_ref[...]) + dot_nn(weight_b, neg_b_ref[...]) + hard * second_embed - total * first_embed
    grad = grad - query_unit * row_sum(query_unit * grad)
    power = jnp.exp(jnp.ceil(jnp.log(query_norm) * (1.0 / log_two)) * log_two).astype(bf16).astype(f32)
    inverse = (16.0 / power).astype(bf16).astype(f32)
    out_ref[0:count] = grad * (power / query_norm)
    out_ref[count : 2 * count] = query_float
    lanes = lax.broadcasted_iota(jnp.int32, (count, 128), 1)
    scalars = jnp.where(lanes == 0, inverse, 0.0)
    for place, value in ((1, total), (3, hard), (5, first_norm), (7, second_norm), (9, positive)):
        high = value.astype(bf16).astype(f32)
        scalars = jnp.where(lanes == place, high, scalars)
        scalars = jnp.where(lanes == place + 1, value - high, scalars)
    line_count = Z * count
    spots = lax.broadcasted_iota(jnp.int32, (count, line_count), 0) + where_ref[0] * count
    spots = jnp.where(spots == lax.broadcasted_iota(jnp.int32, (count, line_count), 1), 1.0, 0.0)
    across = dot_nn(scalars.T[0:16].astype(bf16), spots.astype(bf16))
    out_ref[2 * count : 2 * count + 8, 0:line_count] = across[0:8]
    out_ref[2 * count : 2 * count + 8, line_count : 2 * line_count] = across[8:16]


def node_grad_kernel(own_w_ref, sib_w_ref, own_ref, sib_ref, plane_ref, neg_ref, out_ref, row_ref, neg_w_ref):
    step = pl.program_id(0)
    width = plane_ref.shape[1]
    count = (own_ref.shape[1] - 8) // 2
    line_count = Z * count
    received = (own_ref, sib_ref)

    @pl.when(step == 0)
    def _():
        for side, ref in enumerate(received):
            spread = jnp.sum(ref[:, 2 * count : 2 * count + 8].astype(f32), axis=0)
            scalars = jnp.concatenate([spread[:, :line_count], spread[:, line_count:]], axis=0)
            total = scalars[1:2] + scalars[2:3]
            hard = scalars[3:4] + scalars[4:5]
            row_ref[side, 0:1] = scalars[0:1] * 0.0625
            row_ref[side, 1:2] = -total / (scalars[5:6] + scalars[6:7])
            row_ref[side, 2:3] = hard / (scalars[7:8] + scalars[8:9])
            scores = dot_nt(neg_ref[...], ref[:, count : 2 * count].reshape(line_count, width))
            neg_w_ref[side] = weigh(scores, scalars[9:10] + scalars[10:11])

    negs = neg_ref.shape[0]
    rows = lax.broadcasted_iota(jnp.int32, (OWN, negs), 0) + step * OWN
    spot = jnp.where(rows == lax.broadcasted_iota(jnp.int32, (OWN, negs), 1) * BLOCK + PART, 1.0, 0.0).astype(bf16)
    hood_part = jnp.zeros((OWN, width), f32)
    query_part = jnp.zeros((OWN, width), f32)
    for side, (w_ref, ref) in enumerate(((own_w_ref, own_ref), (sib_w_ref, sib_ref))):
        w_hood = (w_ref[0].astype(f32) * row_ref[side, 0:1]).astype(bf16)
        hood_part = hood_part + dot_nn(w_hood, ref[:, 0:count].reshape(line_count, width))
        w_query = w_ref[1].astype(f32) * row_ref[side, 1:2] + w_ref[2].astype(f32) * row_ref[side, 2:3]
        w_query = (w_query + dot_nn(spot, neg_w_ref[side])).astype(bf16)
        query_part = query_part + dot_nn(w_query, ref[:, count : 2 * count].reshape(line_count, width))
    plane = plane_ref[...].astype(f32)
    place = lax.broadcasted_iota(jnp.int32, (OWN, 1), 0) % BLOCK
    inverse = jnp.where(place == PART, 0.0, 1.0 / (row_sum(plane * plane) + epsilon))
    query_part = query_part - plane * (inverse * row_sum(plane * query_part))
    out_ref[...] = (hood_part + query_part).astype(bf16)


def owner_kernel(pieces_ref, pre_ref, out_ref):
    total = pieces_ref[0].astype(f32)
    for k in range(1, pieces_ref.shape[0]):
        total = total + pieces_ref[k].astype(f32)
    pre = pre_ref[...]
    act = pre * jax.nn.sigmoid(pre)
    norm = row_norm(act)
    unit = act / norm
    place = lax.broadcasted_iota(jnp.int32, (BLOCK, 1), 0)
    back = (total - unit * row_sum(unit * total)) / norm
    total = jnp.where(place == PART, back, total)
    out_ref[...] = (total * silu_slope(pre)).astype(bf16)


def table_kernel(neg_row_ref, grad_ref, projection_ref, out_ref):
    out = dot_nt(grad_ref[...], projection_ref[...])
    rows = lax.broadcasted_iota(jnp.int32, (PART, 1), 0)
    for k in range(X):
        block = out[k * BLOCK : k * BLOCK + PART]
        for i in range(X):
            hit = rows + k * PART == neg_row_ref[i]
            block = block + jnp.where(hit, out[i * BLOCK + PART : i * BLOCK + PART + 1], 0.0)
        out_ref[k * PART : (k + 1) * PART] = block


def call(kernel, out_shape, flops, moved, room, **rest):
    return pl.pallas_call(
        kernel,
        out_shape=out_shape,
        cost_estimate=pl.CostEstimate(flops=flops, bytes_accessed=moved, transcendentals=0),
        compiler_params=pltpu.CompilerParams(vmem_limit_bytes=room << 20),
        **rest,
    )


VMEM = pl.BlockSpec(memory_space=pltpu.VMEM)
SMEM = pl.BlockSpec(memory_space=pltpu.SMEM)


def on_device(feature_table, projection, slot_owner, slot_row, visits, neg_row):
    z, c, x = (lax.axis_index(a) for a in ("z", "c", "x"))
    here = jnp.stack([z, c]).astype(jnp.int32)
    query_count, slot_count = slot_row.shape
    feat_width, embed_width = projection.shape
    line_count = Z * query_count

    pre, shared, negs = call(
        embed_kernel,
        (
            jax.ShapeDtypeStruct((OWN, embed_width), f32),
            jax.ShapeDtypeStruct((OWN, embed_width), bf16),
            jax.ShapeDtypeStruct((8, embed_width), bf16),
        ),
        2 * OWN * embed_width * feat_width,
        5 << 20,
        16,
        in_specs=[SMEM, VMEM, VMEM],
        out_specs=(VMEM, VMEM, VMEM),
    )(neg_row, feature_table, projection)
    plane = lax.all_gather(shared, ("y", "c"), axis=0, tiled=True)
    my_pre = lax.dynamic_slice_in_dim(pre, x * BLOCK, BLOCK, axis=0)

    shifted = jnp.pad(visits, ((0, 0), (3, 0)))
    fields = jnp.concatenate([slot_owner.reshape(query_count, slot_count), slot_row, shifted], axis=1)
    fields = jnp.pad(fields.astype(bf16), ((0, 0), (0, 128 - 3 * slot_count)))
    fields = fields.reshape(8, 4, 128).transpose(1, 0, 2).reshape(4, embed_width)
    block = jnp.concatenate([negs[0:X], fields], axis=0)
    copies = jnp.broadcast_to(block, (Z, 8, embed_width))
    received = lax.all_to_all(copies, "z", split_axis=0, concat_axis=0, tiled=True)
    line_neg = received[:, 0:X].reshape(Z * X, embed_width)
    spread, line = call(
        spread_kernel,
        (
            jax.ShapeDtypeStruct((3, line_count, WIDE), bf16),
            jax.ShapeDtypeStruct((line_count, slot_count), jnp.int32),
        ),
        line_count * WIDE * 48,
        line_count * WIDE * 6,
        56,
        grid=(Z,),
        in_specs=[SMEM, pl.BlockSpec((1, 8, embed_width), lambda i: (i, 0, 0))],
        out_specs=(
            pl.BlockSpec((3, query_count, WIDE), lambda i: (0, i, 0)),
            pl.BlockSpec((query_count, slot_count), lambda i: (i, 0)),
        ),
    )(here, received)
    part = dot_nn(spread.reshape(3 * line_count, WIDE), plane).astype(bf16)
    part, plane, line, line_neg = lax.optimization_barrier((part, plane, line, line_neg))
    got = lax.psum_scatter(
        part.reshape(3, line_count, embed_width), "z", scatter_dimension=1, tiled=True
    )

    core_plane = lax.dynamic_index_in_dim(plane.reshape(Y, C, X, BLOCK, embed_width), c, axis=1, keepdims=False)
    core_plane = core_plane.transpose(1, 0, 2, 3)
    core_neg = core_plane[:, :, PART].reshape(X * Y, embed_width)
    core_plane = core_plane.reshape(NARROW, embed_width)
    some_neg = lax.all_gather(line_neg, "y", axis=0, tiled=True)
    other_neg = lax.ppermute(some_neg, "c", SIBLING)
    line_sib = lax.ppermute(line, "c", SIBLING)

    def node_weights(some_line):
        return call(
            node_weights_kernel,
            jax.ShapeDtypeStruct((3, NARROW, line_count), bf16),
            line_count * NARROW * 48,
            line_count * NARROW * 6,
            12,
            grid=(X,),
            in_specs=[SMEM, pl.BlockSpec((slot_count, line_count), lambda i: (0, 0))],
            out_specs=pl.BlockSpec((3, OWN, line_count), lambda i: (0, i, 0)),
        )(here, some_line.T)

    own_w, sib_w = node_weights(line), node_weights(line_sib)
    got, own_w, sib_w, core_plane, core_neg, some_neg, other_neg, my_pre = lax.optimization_barrier(
        (got, own_w, sib_w, core_plane, core_neg, some_neg, other_neg, my_pre)
    )

    payload_rows = 2 * query_count + 8
    payload = call(
        query_kernel,
        jax.ShapeDtypeStruct((payload_rows, embed_width), f32),
        4 * query_count * 512 * embed_width,
        1 << 20,
        10,
        in_specs=[SMEM] + [VMEM] * 3,
        out_specs=VMEM,
    )(here, got, some_neg, other_neg)
    own = lax.all_gather(payload.astype(f16), "z", axis=0, tiled=True).astype(bf16)
    own = own.reshape(Z, payload_rows, embed_width)
    sib = lax.ppermute(own, "c", SIBLING)

    node_grads = call(
        node_grad_kernel,
        jax.ShapeDtypeStruct((NARROW, embed_width), bf16),
        8 * line_count * NARROW * embed_width,
        16 << 20,
        36,
        grid=(X,),
        in_specs=[
            pl.BlockSpec((3, OWN, line_count), lambda i: (0, i, 0)),
            pl.BlockSpec((3, OWN, line_count), lambda i: (0, i, 0)),
            pl.BlockSpec((Z, payload_rows, embed_width), lambda i: (0, 0, 0)),
            pl.BlockSpec((Z, payload_rows, embed_width), lambda i: (0, 0, 0)),
            pl.BlockSpec((OWN, embed_width), lambda i: (i, 0)),
            pl.BlockSpec((X * Y, embed_width), lambda i: (0, 0)),
        ],
        out_specs=pl.BlockSpec((OWN, embed_width), lambda i: (i, 0)),
        scratch_shapes=[pltpu.VMEM((2, 8, line_count), f32), pltpu.VMEM((2, X * Y, line_count), bf16)],
    )(own_w, sib_w, own, sib, core_plane, core_neg)

    pieces = lax.all_to_all(node_grads, ("x", "y"), split_axis=0, concat_axis=0, tiled=True)
    pre_grad = call(
        owner_kernel,
        jax.ShapeDtypeStruct((BLOCK, embed_width), bf16),
        1 << 22,
        3 << 20,
        10,
        in_specs=[VMEM] * 2,
        out_specs=VMEM,
    )(pieces.reshape(X * Y, BLOCK, embed_width), my_pre)
    all_pre_grad = lax.all_gather(pre_grad, "x", axis=0, tiled=True)
    return call(
        table_kernel,
        jax.ShapeDtypeStruct((ROWS, feat_width), f32),
        2 * OWN * embed_width * feat_width,
        4 << 20,
        16,
        in_specs=[SMEM, VMEM, VMEM],
        out_specs=VMEM,
    )(neg_row, all_pre_grad, projection)


def solution(mesh):
    grid = Mesh(mesh.devices.reshape(Y, Z, C, X), ("y", "z", "c", "x"))
    shard = ("y", "z", "c")
    every = ("y", "z", "c", "x")
    return jax.shard_map(
        on_device,
        mesh=grid,
        in_specs=(
            P(shard, None),
            P(),
            P(every, None, None),
            P(every, None),
            P(every, None),
            P(shard),
        ),
        out_specs=P(shard, None),
        check_vma=False,
    )
```

```python
import jax
import jax.numpy as jnp
from jax import lax
from jax.experimental import pallas as pl
from jax.experimental.pallas import tpu as pltpu
from jax.sharding import Mesh
from jax.sharding import PartitionSpec as P

score_scale = 8.0
margin_value = 0.1
epsilon = 1e-06
log_two = 0.6931471805599453

Y, Z, C, X = 4, 16, 2, 4
ROWS = 256
PART = ROWS // X
BLOCK = PART + 8
OWN = X * BLOCK
WIDE = Y * C * OWN
NARROW = Y * OWN
bf16 = jnp.bfloat16
f16 = jnp.float16
f32 = jnp.float32
SIBLING = [(0, 1), (1, 0)]


def silu_slope(preact):
    gate_value = jax.nn.sigmoid(preact)
    return gate_value * (1.0 + preact * (1.0 - gate_value))


def row_sum(values):
    return jnp.sum(values, axis=1, keepdims=True)


def row_norm(values):
    return jnp.sqrt(row_sum(values * values) + epsilon)


def weigh(score, positive):
    return (score_scale * jax.nn.sigmoid(score_scale * (score - positive + margin_value))).astype(bf16)


def dot_nn(left, right):
    return lax.dot_general(left, right, (((1,), (0,)), ((), ())), preferred_element_type=f32)


def dot_nt(left, right):
    return lax.dot_general(left, right, (((1,), (1,)), ((), ())), preferred_element_type=f32)


def decode(packed, axis):
    owner = packed & 127
    row = (packed >> 7) & 255
    visits = (packed >> 15).astype(f32)
    coefs = visits / jnp.sum(visits, axis=axis, keepdims=True)
    return owner >> 5, owner & 1, (owner >> 1) & 15, row >> 6, row & 63, coefs


def embed_kernel(neg_row_ref, table_hbm, projection_hbm, pre_ref, shared_ref, negs_ref, table_ref, projection_ref, sems):
    loads = (
        pltpu.make_async_copy(table_hbm, table_ref, sems.at[0]),
        pltpu.make_async_copy(projection_hbm, projection_ref, sems.at[1]),
    )
    for load in loads:
        load.start()
    picks = lax.broadcasted_iota(jnp.int32, (X * 8, ROWS), 0)
    cols = lax.broadcasted_iota(jnp.int32, (X * 8, ROWS), 1)
    hot = jnp.zeros((X * 8, ROWS), f32)
    for i in range(X):
        hot = hot + jnp.where((picks == 8 * i) & (cols == neg_row_ref[i]), 1.0, 0.0)
    for load in loads:
        load.wait()
    neg_rows = dot_nn(hot.astype(bf16), table_ref[...]).astype(bf16)
    neg_pre = dot_nn(neg_rows, projection_ref[...])
    neg_act = neg_pre * jax.nn.sigmoid(neg_pre)
    neg_unit = (neg_act / row_norm(neg_act)).astype(bf16)
    source = lax.broadcasted_iota(jnp.int32, (8, X * 8), 0) * 8
    pick = jnp.where(source == lax.broadcasted_iota(jnp.int32, (8, X * 8), 1), 1.0, 0.0)
    negs_ref[...] = dot_nn(pick.astype(bf16), neg_unit).astype(bf16)
    for i in range(X):
        node_pre = dot_nn(table_ref[i * PART : (i + 1) * PART], projection_ref[...])
        start = i * BLOCK
        pre_ref[start : start + PART] = node_pre
        pre_ref[start + PART : start + BLOCK] = neg_pre[8 * i : 8 * i + 8]
        shared_ref[start : start + PART] = (node_pre * jax.nn.sigmoid(node_pre)).astype(bf16)
        shared_ref[start + PART : start + BLOCK] = neg_unit[8 * i : 8 * i + 8]


def spread_kernel(where_ref, received_ref, out_ref, line_ref):
    rows, slots = line_ref.shape
    tiles = [received_ref[0, X:8, t * 128 : (t + 1) * 128].astype(f32) for t in range(8)]
    fields = jnp.concatenate(tiles, axis=0)
    packed = fields[:, 0:slots] + fields[:, slots : 2 * slots] * 128.0 + fields[:, 2 * slots : 3 * slots] * 32768.0
    packed = packed.astype(jnp.int32)
    line_ref[...] = packed
    ny, nc, nz, part, rest, coefs = decode(packed, 1)
    column = jnp.where(nz == where_ref[0], (ny * C + nc) * OWN + part * BLOCK + rest, -1)
    high, low = column >> 8, column & 255
    lanes = lax.broadcasted_iota(jnp.int32, (rows, 256), 1)
    chunks = WIDE // 256
    totals = [jnp.zeros((rows, 256), bf16) for _ in range(chunks)]
    nothing = jnp.zeros((rows, 256), bf16)
    for slot in range(slots):
        weight = coefs[:, slot : slot + 1] if slot > 2 else 1.0
        hot = jnp.where(lanes == low[:, slot : slot + 1], weight, 0.0).astype(bf16)
        level = jnp.broadcast_to(high[:, slot : slot + 1].astype(f32), (rows, 256)).astype(bf16)
        for k in range(chunks):
            term = jnp.where(level == k, hot, nothing)
            if slot == 1 or slot == 2:
                out_ref[slot, :, k * 256 : (k + 1) * 256] = term
            else:
                totals[k] = totals[k] + term
    for k in range(chunks):
        out_ref[0, :, k * 256 : (k + 1) * 256] = totals[k]


def node_weights_kernel(where_ref, line_ref, out_ref):
    ny, nc, nz, part, rest, coefs = decode(line_ref[...], 0)
    here = (nz == where_ref[0]) & (nc == where_ref[1])
    column = jnp.where(here, part * (Y * BLOCK) + ny * BLOCK + rest, -1)
    slots, count = column.shape
    base = pl.program_id(0) * OWN
    chunk = 32
    for k in range(OWN // chunk):
        nodes = lax.broadcasted_iota(jnp.int32, (chunk, count), 0) + (base + k * chunk)
        total = jnp.where(nodes == column[0:1], 1.0, 0.0)
        for slot in range(3, slots):
            total = total + jnp.where(nodes == column[slot : slot + 1], coefs[slot : slot + 1], 0.0)
        span = pl.ds(k * chunk, chunk)
        out_ref[0, span, :] = total.astype(bf16)
        out_ref[1, span, :] = jnp.where(nodes == column[1:2], 1.0, 0.0).astype(bf16)
        out_ref[2, span, :] = jnp.where(nodes == column[2:3], 1.0, 0.0).astype(bf16)


def query_kernel(got_ref, neg_a_ref, neg_b_ref, out_ref):
    count, width = got_ref.shape[1:]
    hood = got_ref[0].astype(f32)
    query_norm = row_norm(hood)
    query_unit = hood / query_norm
    query_embed = query_unit.astype(bf16)
    query_float = query_embed.astype(f32)
    first = got_ref[1].astype(f32)
    second = got_ref[2].astype(f32)
    first_norm, second_norm = row_norm(first), row_norm(second)
    first_embed = (first / first_norm).astype(bf16).astype(f32)
    second_embed = (second / second_norm).astype(bf16).astype(f32)
    positive = row_sum(query_float * first_embed)
    hard = weigh(row_sum(query_float * second_embed), positive).astype(f32)
    weight_a = weigh(dot_nt(query_embed, neg_a_ref[...]), positive)
    weight_b = weigh(dot_nt(query_embed, neg_b_ref[...]), positive)
    total = row_sum(weight_a.astype(f32)) + row_sum(weight_b.astype(f32)) + hard
    grad = dot_nn(weight_a, neg_a_ref[...]) + dot_nn(weight_b, neg_b_ref[...]) + hard * second_embed - total * first_embed
    grad = grad - query_unit * row_sum(query_unit * grad)
    power = jnp.exp(jnp.ceil(jnp.log(query_norm) * (1.0 / log_two)) * log_two).astype(bf16).astype(f32)
    inverse = (16.0 / power).astype(bf16).astype(f32)
    out_ref[:, 0:width] = grad * (power / query_norm)
    out_ref[:, width : 2 * width] = query_float
    lanes = lax.broadcasted_iota(jnp.int32, (count, 128), 1)
    scalars = jnp.where(lanes == 0, inverse, 0.0)
    for place, value in ((1, total), (3, hard), (5, first_norm), (7, second_norm), (9, positive)):
        high = value.astype(bf16).astype(f32)
        scalars = jnp.where(lanes == place, high, scalars)
        scalars = jnp.where(lanes == place + 1, value - high, scalars)
    out_ref[:, 2 * width :] = scalars


def node_grad_kernel(own_w_ref, sib_w_ref, own_ref, sib_ref, plane_ref, neg_ref, out_ref, row_ref, neg_w_ref):
    step = pl.program_id(0)
    width = plane_ref.shape[1]
    received = (own_ref, sib_ref)

    @pl.when(step == 0)
    def _():
        for side, ref in enumerate(received):
            scalars = ref[:, 2 * width :].astype(f32).T
            total = scalars[1:2] + scalars[2:3]
            hard = scalars[3:4] + scalars[4:5]
            row_ref[side, 0:1] = scalars[0:1] * 0.0625
            row_ref[side, 1:2] = -total / (scalars[5:6] + scalars[6:7])
            row_ref[side, 2:3] = hard / (scalars[7:8] + scalars[8:9])
            scores = dot_nt(neg_ref[...], ref[:, width : 2 * width])
            neg_w_ref[side] = weigh(scores, scalars[9:10] + scalars[10:11])

    negs = neg_ref.shape[0]
    rows = lax.broadcasted_iota(jnp.int32, (OWN, negs), 0) + step * OWN
    spot = jnp.where(rows == lax.broadcasted_iota(jnp.int32, (OWN, negs), 1) * BLOCK + PART, 1.0, 0.0).astype(bf16)
    hood_part = jnp.zeros((OWN, width), f32)
    query_part = jnp.zeros((OWN, width), f32)
    for side, (w_ref, ref) in enumerate(((own_w_ref, own_ref), (sib_w_ref, sib_ref))):
        w_hood = (w_ref[0].astype(f32) * row_ref[side, 0:1]).astype(bf16)
        hood_part = hood_part + dot_nn(w_hood, ref[:, 0:width])
        w_query = w_ref[1].astype(f32) * row_ref[side, 1:2] + w_ref[2].astype(f32) * row_ref[side, 2:3]
        w_query = (w_query + dot_nn(spot, neg_w_ref[side])).astype(bf16)
        query_part = query_part + dot_nn(w_query, ref[:, width : 2 * width])
    plane = plane_ref[...].astype(f32)
    place = lax.broadcasted_iota(jnp.int32, (OWN, 1), 0) % BLOCK
    inverse = jnp.where(place == PART, 0.0, 1.0 / (row_sum(plane * plane) + epsilon))
    query_part = query_part - plane * (inverse * row_sum(plane * query_part))
    out_ref[...] = (hood_part + query_part).astype(bf16)


def owner_kernel(pieces_ref, pre_ref, out_ref):
    total = pieces_ref[0].astype(f32)
    for k in range(1, pieces_ref.shape[0]):
        total = total + pieces_ref[k].astype(f32)
    pre = pre_ref[...]
    act = pre * jax.nn.sigmoid(pre)
    norm = row_norm(act)
    unit = act / norm
    place = lax.broadcasted_iota(jnp.int32, (BLOCK, 1), 0)
    back = (total - unit * row_sum(unit * total)) / norm
    total = jnp.where(place == PART, back, total)
    out_ref[...] = (total * silu_slope(pre)).astype(bf16)


def table_kernel(neg_row_ref, grad_ref, projection_ref, out_ref):
    out = dot_nt(grad_ref[...], projection_ref[...])
    rows = lax.broadcasted_iota(jnp.int32, (PART, 1), 0)
    for k in range(X):
        block = out[k * BLOCK : k * BLOCK + PART]
        for i in range(X):
            hit = rows + k * PART == neg_row_ref[i]
            block = block + jnp.where(hit, out[i * BLOCK + PART : i * BLOCK + PART + 1], 0.0)
        out_ref[k * PART : (k + 1) * PART] = block


def call(kernel, out_shape, flops, moved, room, **rest):
    return pl.pallas_call(
        kernel,
        out_shape=out_shape,
        cost_estimate=pl.CostEstimate(flops=flops, bytes_accessed=moved, transcendentals=0),
        compiler_params=pltpu.CompilerParams(vmem_limit_bytes=room << 20),
        **rest,
    )


VMEM = pl.BlockSpec(memory_space=pltpu.VMEM)
SMEM = pl.BlockSpec(memory_space=pltpu.SMEM)


def on_device(feature_table, projection, slot_owner, slot_row, visits, neg_row):
    z, c, x = (lax.axis_index(a) for a in ("z", "c", "x"))
    here = jnp.stack([z, c]).astype(jnp.int32)
    query_count, slot_count = slot_row.shape
    feat_width, embed_width = projection.shape
    line_count = Z * query_count

    pre, shared, negs = call(
        embed_kernel,
        (
            jax.ShapeDtypeStruct((OWN, embed_width), f32),
            jax.ShapeDtypeStruct((OWN, embed_width), bf16),
            jax.ShapeDtypeStruct((8, embed_width), bf16),
        ),
        2 * OWN * embed_width * feat_width,
        5 << 20,
        56,
        in_specs=[SMEM, pl.BlockSpec(memory_space=pl.ANY), pl.BlockSpec(memory_space=pl.ANY)],
        out_specs=(VMEM, VMEM, VMEM),
        scratch_shapes=[
            pltpu.VMEM((ROWS, feat_width), bf16),
            pltpu.VMEM((feat_width, embed_width), bf16),
            pltpu.SemaphoreType.DMA((2,)),
        ],
    )(neg_row, feature_table, projection)
    plane = lax.all_gather(shared, ("y", "c"), axis=0, tiled=True)
    my_pre = lax.dynamic_slice_in_dim(pre, x * BLOCK, BLOCK, axis=0)

    shifted = jnp.pad(visits, ((0, 0), (3, 0)))
    fields = jnp.concatenate([slot_owner.reshape(query_count, slot_count), slot_row, shifted], axis=1)
    fields = jnp.pad(fields.astype(bf16), ((0, 0), (0, 128 - 3 * slot_count)))
    fields = fields.reshape(8, 4, 128).transpose(1, 0, 2).reshape(4, embed_width)
    block = jnp.concatenate([negs[0:X], fields], axis=0)
    copies = jnp.broadcast_to(block, (Z, 8, embed_width))
    received = lax.all_to_all(copies, "z", split_axis=0, concat_axis=0, tiled=True)
    line_neg = received[:, 0:X].reshape(Z * X, embed_width)
    spread, line = call(
        spread_kernel,
        (
            jax.ShapeDtypeStruct((3, line_count, WIDE), bf16),
            jax.ShapeDtypeStruct((line_count, slot_count), jnp.int32),
        ),
        line_count * WIDE * 48,
        line_count * WIDE * 6,
        56,
        grid=(Z,),
        in_specs=[SMEM, pl.BlockSpec((1, 8, embed_width), lambda i: (i, 0, 0))],
        out_specs=(
            pl.BlockSpec((3, query_count, WIDE), lambda i: (0, i, 0)),
            pl.BlockSpec((query_count, slot_count), lambda i: (i, 0)),
        ),
    )(here, received)
    part = dot_nn(spread.reshape(3 * line_count, WIDE), plane).astype(bf16)
    part, plane, line, line_neg = lax.optimization_barrier((part, plane, line, line_neg))
    got = lax.psum_scatter(
        part.reshape(3, line_count, embed_width), "z", scatter_dimension=1, tiled=True
    )

    core_plane = lax.dynamic_index_in_dim(plane.reshape(Y, C, X, BLOCK, embed_width), c, axis=1, keepdims=False)
    core_plane = core_plane.transpose(1, 0, 2, 3)
    core_neg = core_plane[:, :, PART].reshape(X * Y, embed_width)
    core_plane = core_plane.reshape(NARROW, embed_width)
    some_neg = lax.all_gather(line_neg, "y", axis=0, tiled=True)
    other_neg = lax.ppermute(some_neg, "c", SIBLING)
    line_sib = lax.ppermute(line, "c", SIBLING)

    def node_weights(some_line):
        return call(
            node_weights_kernel,
            jax.ShapeDtypeStruct((3, NARROW, line_count), bf16),
            line_count * NARROW * 48,
            line_count * NARROW * 6,
            12,
            grid=(X,),
            in_specs=[SMEM, pl.BlockSpec((slot_count, line_count), lambda i: (0, 0))],
            out_specs=pl.BlockSpec((3, OWN, line_count), lambda i: (0, i, 0)),
        )(here, some_line.T)

    own_w, sib_w = node_weights(line), node_weights(line_sib)
    got, own_w, sib_w, core_plane, core_neg, some_neg, other_neg, my_pre = lax.optimization_barrier(
        (got, own_w, sib_w, core_plane, core_neg, some_neg, other_neg, my_pre)
    )

    payload_width = 2 * embed_width + 128
    payload = call(
        query_kernel,
        jax.ShapeDtypeStruct((query_count, payload_width), f32),
        4 * query_count * 512 * embed_width,
        1 << 20,
        10,
        in_specs=[VMEM] * 3,
        out_specs=VMEM,
    )(got, some_neg, other_neg)
    own = lax.all_gather(payload.astype(f16), "z", axis=0, tiled=True).astype(bf16)
    sib = lax.ppermute(own, "c", SIBLING)

    node_grads = call(
        node_grad_kernel,
        jax.ShapeDtypeStruct((NARROW, embed_width), bf16),
        8 * line_count * NARROW * embed_width,
        16 << 20,
        36,
        grid=(X,),
        in_specs=[
            pl.BlockSpec((3, OWN, line_count), lambda i: (0, i, 0)),
            pl.BlockSpec((3, OWN, line_count), lambda i: (0, i, 0)),
            pl.BlockSpec((line_count, payload_width), lambda i: (0, 0)),
            pl.BlockSpec((line_count, payload_width), lambda i: (0, 0)),
            pl.BlockSpec((OWN, embed_width), lambda i: (i, 0)),
            pl.BlockSpec((X * Y, embed_width), lambda i: (0, 0)),
        ],
        out_specs=pl.BlockSpec((OWN, embed_width), lambda i: (i, 0)),
        scratch_shapes=[pltpu.VMEM((2, 8, line_count), f32), pltpu.VMEM((2, X * Y, line_count), bf16)],
    )(own_w, sib_w, own, sib, core_plane, core_neg)

    pieces = lax.all_to_all(node_grads, ("x", "y"), split_axis=0, concat_axis=0, tiled=True)
    pre_grad = call(
        owner_kernel,
        jax.ShapeDtypeStruct((BLOCK, embed_width), bf16),
        1 << 22,
        3 << 20,
        10,
        in_specs=[VMEM] * 2,
        out_specs=VMEM,
    )(pieces.reshape(X * Y, BLOCK, embed_width), my_pre)
    all_pre_grad = lax.all_gather(pre_grad, "x", axis=0, tiled=True)
    return call(
        table_kernel,
        jax.ShapeDtypeStruct((ROWS, feat_width), f32),
        2 * OWN * embed_width * feat_width,
        4 << 20,
        16,
        in_specs=[SMEM, VMEM, VMEM],
        out_specs=VMEM,
    )(neg_row, all_pre_grad, projection)


def solution(mesh):
    grid = Mesh(mesh.devices.reshape(Y, Z, C, X), ("y", "z", "c", "x"))
    shard = ("y", "z", "c")
    every = ("y", "z", "c", "x")
    return jax.shard_map(
        on_device,
        mesh=grid,
        in_specs=(
            P(shard, None),
            P(),
            P(every, None, None),
            P(every, None),
            P(every, None),
            P(shard),
        ),
        out_specs=P(shard, None),
        check_vma=False,
    )
```

```python
import jax
import jax.numpy as jnp
from jax import lax
from jax.experimental import pallas as pl
from jax.experimental.pallas import tpu as pltpu
from jax.sharding import Mesh
from jax.sharding import PartitionSpec as P

score_scale = 8.0
margin_value = 0.1
epsilon = 1e-06
log_two = 0.6931471805599453

Y, Z, C, X = 4, 16, 2, 4
ROWS = 256
PART = ROWS // X
BLOCK = PART + 8
OWN = X * BLOCK
WIDE = Y * C * OWN
NARROW = Y * OWN
bf16 = jnp.bfloat16
f16 = jnp.float16
f32 = jnp.float32
SIBLING = [(0, 1), (1, 0)]


def silu_slope(preact):
    gate_value = jax.nn.sigmoid(preact)
    return gate_value * (1.0 + preact * (1.0 - gate_value))


def row_sum(values):
    return jnp.sum(values, axis=1, keepdims=True)


def row_norm(values):
    return jnp.sqrt(row_sum(values * values) + epsilon)


def weigh(score, positive):
    return (score_scale * jax.nn.sigmoid(score_scale * (score - positive + margin_value))).astype(bf16)


def dot_nn(left, right):
    return lax.dot_general(left, right, (((1,), (0,)), ((), ())), preferred_element_type=f32)


def dot_nt(left, right):
    return lax.dot_general(left, right, (((1,), (1,)), ((), ())), preferred_element_type=f32)


def decode(packed, axis):
    owner = packed & 127
    row = (packed >> 7) & 255
    visits = (packed >> 15).astype(f32)
    coefs = visits / jnp.sum(visits, axis=axis, keepdims=True)
    return owner >> 5, owner & 1, (owner >> 1) & 15, row >> 6, row & 63, coefs


def embed_kernel(neg_row_ref, table_hbm, projection_hbm, pre_ref, shared_ref, negs_ref, table_ref, projection_ref, sems):
    loads = (
        pltpu.make_async_copy(table_hbm, table_ref, sems.at[0]),
        pltpu.make_async_copy(projection_hbm, projection_ref, sems.at[1]),
    )
    for load in loads:
        load.start()
    picks = lax.broadcasted_iota(jnp.int32, (X * 8, ROWS), 0)
    cols = lax.broadcasted_iota(jnp.int32, (X * 8, ROWS), 1)
    hot = jnp.zeros((X * 8, ROWS), f32)
    for i in range(X):
        hot = hot + jnp.where((picks == 8 * i) & (cols == neg_row_ref[i]), 1.0, 0.0)
    for load in loads:
        load.wait()
    neg_rows = dot_nn(hot.astype(bf16), table_ref[...]).astype(bf16)
    neg_pre = dot_nn(neg_rows, projection_ref[...])
    neg_act = neg_pre * jax.nn.sigmoid(neg_pre)
    neg_unit = (neg_act / row_norm(neg_act)).astype(bf16)
    source = lax.broadcasted_iota(jnp.int32, (8, X * 8), 0) * 8
    pick = jnp.where(source == lax.broadcasted_iota(jnp.int32, (8, X * 8), 1), 1.0, 0.0)
    negs_ref[...] = dot_nn(pick.astype(bf16), neg_unit).astype(bf16)
    for i in range(X):
        node_pre = dot_nn(table_ref[i * PART : (i + 1) * PART], projection_ref[...])
        start = i * BLOCK
        pre_ref[start : start + PART] = node_pre
        pre_ref[start + PART : start + BLOCK] = neg_pre[8 * i : 8 * i + 8]
        shared_ref[start : start + PART] = (node_pre * jax.nn.sigmoid(node_pre)).astype(bf16)
        shared_ref[start + PART : start + BLOCK] = neg_unit[8 * i : 8 * i + 8]


def spread_kernel(where_ref, received_ref, out_ref, line_ref):
    rows, slots = line_ref.shape
    tiles = [received_ref[0, X:8, t * 128 : (t + 1) * 128].astype(f32) for t in range(8)]
    fields = jnp.concatenate(tiles, axis=0)
    packed = fields[:, 0:slots] + fields[:, slots : 2 * slots] * 128.0 + fields[:, 2 * slots : 3 * slots] * 32768.0
    packed = packed.astype(jnp.int32)
    line_ref[...] = packed
    ny, nc, nz, part, rest, coefs = decode(packed, 1)
    column = jnp.where(nz == where_ref[0], (ny * C + nc) * OWN + part * BLOCK + rest, -1)
    high, low = column >> 8, column & 255
    lanes = lax.broadcasted_iota(jnp.int32, (rows, 256), 1)
    chunks = WIDE // 256
    totals = [jnp.zeros((rows, 256), bf16) for _ in range(chunks)]
    nothing = jnp.zeros((rows, 256), bf16)
    for slot in range(slots):
        weight = coefs[:, slot : slot + 1] if slot > 2 else 1.0
        hot = jnp.where(lanes == low[:, slot : slot + 1], weight, 0.0).astype(bf16)
        level = jnp.broadcast_to(high[:, slot : slot + 1].astype(f32), (rows, 256)).astype(bf16)
        for k in range(chunks):
            term = jnp.where(level == k, hot, nothing)
            if slot == 1 or slot == 2:
                out_ref[slot, :, k * 256 : (k + 1) * 256] = term
            else:
                totals[k] = totals[k] + term
    for k in range(chunks):
        out_ref[0, :, k * 256 : (k + 1) * 256] = totals[k]


def node_weights_kernel(where_ref, line_ref, out_ref):
    ny, nc, nz, part, rest, coefs = decode(line_ref[...], 0)
    here = (nz == where_ref[0]) & (nc == where_ref[1])
    column = jnp.where(here, part * (Y * BLOCK) + ny * BLOCK + rest, -1)
    slots, count = column.shape
    base = pl.program_id(0) * OWN
    chunk = 32
    for k in range(OWN // chunk):
        nodes = lax.broadcasted_iota(jnp.int32, (chunk, count), 0) + (base + k * chunk)
        total = jnp.where(nodes == column[0:1], 1.0, 0.0)
        for slot in range(3, slots):
            total = total + jnp.where(nodes == column[slot : slot + 1], coefs[slot : slot + 1], 0.0)
        span = pl.ds(k * chunk, chunk)
        out_ref[0, span, :] = total.astype(bf16)
        out_ref[1, span, :] = jnp.where(nodes == column[1:2], 1.0, 0.0).astype(bf16)
        out_ref[2, span, :] = jnp.where(nodes == column[2:3], 1.0, 0.0).astype(bf16)


def query_kernel(got_ref, neg_a_ref, neg_b_ref, out_ref):
    count, width = got_ref.shape[1:]
    hood = got_ref[0].astype(f32)
    query_norm = row_norm(hood)
    query_unit = hood / query_norm
    query_embed = query_unit.astype(bf16)
    query_float = query_embed.astype(f32)
    first = got_ref[1].astype(f32)
    second = got_ref[2].astype(f32)
    first_norm, second_norm = row_norm(first), row_norm(second)
    first_embed = (first / first_norm).astype(bf16).astype(f32)
    second_embed = (second / second_norm).astype(bf16).astype(f32)
    positive = row_sum(query_float * first_embed)
    hard = weigh(row_sum(query_float * second_embed), positive).astype(f32)
    weight_a = weigh(dot_nt(query_embed, neg_a_ref[...]), positive)
    weight_b = weigh(dot_nt(query_embed, neg_b_ref[...]), positive)
    total = row_sum(weight_a.astype(f32)) + row_sum(weight_b.astype(f32)) + hard
    grad = dot_nn(weight_a, neg_a_ref[...]) + dot_nn(weight_b, neg_b_ref[...]) + hard * second_embed - total * first_embed
    grad = grad - query_unit * row_sum(query_unit * grad)
    power = jnp.exp(jnp.ceil(jnp.log(query_norm) * (1.0 / log_two)) * log_two).astype(bf16).astype(f32)
    inverse = (16.0 / power).astype(bf16).astype(f32)
    out_ref[:, 0:width] = grad * (power / query_norm)
    out_ref[:, width : 2 * width] = query_float
    lanes = lax.broadcasted_iota(jnp.int32, (count, 128), 1)
    scalars = jnp.where(lanes == 0, inverse, 0.0)
    for place, value in ((1, total), (3, hard), (5, first_norm), (7, second_norm), (9, positive)):
        high = value.astype(bf16).astype(f32)
        scalars = jnp.where(lanes == place, high, scalars)
        scalars = jnp.where(lanes == place + 1, value - high, scalars)
    out_ref[:, 2 * width :] = scalars


def node_grad_kernel(*refs):
    weight_ref, ref, plane_ref, neg_ref = refs[:4]
    out_ref, row_ref, neg_w_ref = refs[-3:]
    step = pl.program_id(0)
    width = plane_ref.shape[1]

    @pl.when(step == 0)
    def _():
        scalars = ref[:, 2 * width :].astype(f32).T
        total = scalars[1:2] + scalars[2:3]
        hard = scalars[3:4] + scalars[4:5]
        row_ref[0:1] = scalars[0:1] * 0.0625
        row_ref[1:2] = -total / (scalars[5:6] + scalars[6:7])
        row_ref[2:3] = hard / (scalars[7:8] + scalars[8:9])
        scores = dot_nt(neg_ref[...], ref[:, width : 2 * width])
        neg_w_ref[...] = weigh(scores, scalars[9:10] + scalars[10:11])

    negs = neg_ref.shape[0]
    rows = lax.broadcasted_iota(jnp.int32, (OWN, negs), 0) + step * OWN
    spot = jnp.where(rows == lax.broadcasted_iota(jnp.int32, (OWN, negs), 1) * BLOCK + PART, 1.0, 0.0).astype(bf16)
    w_hood = (weight_ref[0].astype(f32) * row_ref[0:1]).astype(bf16)
    hood_part = dot_nn(w_hood, ref[:, 0:width])
    w_query = weight_ref[1].astype(f32) * row_ref[1:2] + weight_ref[2].astype(f32) * row_ref[2:3]
    w_query = (w_query + dot_nn(spot, neg_w_ref[...])).astype(bf16)
    query_part = dot_nn(w_query, ref[:, width : 2 * width])
    plane = plane_ref[...].astype(f32)
    place = lax.broadcasted_iota(jnp.int32, (OWN, 1), 0) % BLOCK
    inverse = jnp.where(place == PART, 0.0, 1.0 / (row_sum(plane * plane) + epsilon))
    query_part = query_part - plane * (inverse * row_sum(plane * query_part))
    result = hood_part + query_part
    if len(refs) > 7:
        result = result + refs[4][...]
    out_ref[...] = result.astype(out_ref.dtype)


def owner_kernel(pieces_ref, pre_ref, out_ref):
    total = pieces_ref[0].astype(f32)
    for k in range(1, pieces_ref.shape[0]):
        total = total + pieces_ref[k].astype(f32)
    pre = pre_ref[...]
    act = pre * jax.nn.sigmoid(pre)
    norm = row_norm(act)
    unit = act / norm
    place = lax.broadcasted_iota(jnp.int32, (BLOCK, 1), 0)
    back = (total - unit * row_sum(unit * total)) / norm
    total = jnp.where(place == PART, back, total)
    out_ref[...] = (total * silu_slope(pre)).astype(bf16)


def table_kernel(neg_row_ref, grad_ref, projection_ref, out_ref):
    out = dot_nt(grad_ref[...], projection_ref[...])
    rows = lax.broadcasted_iota(jnp.int32, (PART, 1), 0)
    for k in range(X):
        block = out[k * BLOCK : k * BLOCK + PART]
        for i in range(X):
            hit = rows + k * PART == neg_row_ref[i]
            block = block + jnp.where(hit, out[i * BLOCK + PART : i * BLOCK + PART + 1], 0.0)
        out_ref[k * PART : (k + 1) * PART] = block


def call(kernel, out_shape, flops, moved, room, **rest):
    return pl.pallas_call(
        kernel,
        out_shape=out_shape,
        cost_estimate=pl.CostEstimate(flops=flops, bytes_accessed=moved, transcendentals=0),
        compiler_params=pltpu.CompilerParams(vmem_limit_bytes=room << 20),
        **rest,
    )


VMEM = pl.BlockSpec(memory_space=pltpu.VMEM)
SMEM = pl.BlockSpec(memory_space=pltpu.SMEM)


def on_device(feature_table, projection, slot_owner, slot_row, visits, neg_row):
    z, c, x = (lax.axis_index(a) for a in ("z", "c", "x"))
    here = jnp.stack([z, c]).astype(jnp.int32)
    query_count, slot_count = slot_row.shape
    feat_width, embed_width = projection.shape
    line_count = Z * query_count

    pre, shared, negs = call(
        embed_kernel,
        (
            jax.ShapeDtypeStruct((OWN, embed_width), f32),
            jax.ShapeDtypeStruct((OWN, embed_width), bf16),
            jax.ShapeDtypeStruct((8, embed_width), bf16),
        ),
        2 * OWN * embed_width * feat_width,
        5 << 20,
        56,
        in_specs=[SMEM, pl.BlockSpec(memory_space=pl.ANY), pl.BlockSpec(memory_space=pl.ANY)],
        out_specs=(VMEM, VMEM, VMEM),
        scratch_shapes=[
            pltpu.VMEM((ROWS, feat_width), bf16),
            pltpu.VMEM((feat_width, embed_width), bf16),
            pltpu.SemaphoreType.DMA((2,)),
        ],
    )(neg_row, feature_table, projection)
    plane = lax.all_gather(shared, ("y", "c"), axis=0, tiled=True)
    my_pre = lax.dynamic_slice_in_dim(pre, x * BLOCK, BLOCK, axis=0)

    shifted = jnp.pad(visits, ((0, 0), (3, 0)))
    fields = jnp.concatenate([slot_owner.reshape(query_count, slot_count), slot_row, shifted], axis=1)
    fields = jnp.pad(fields.astype(bf16), ((0, 0), (0, 128 - 3 * slot_count)))
    fields = fields.reshape(8, 4, 128).transpose(1, 0, 2).reshape(4, embed_width)
    block = jnp.concatenate([negs[0:X], fields], axis=0)
    copies = jnp.broadcast_to(block, (Z, 8, embed_width))
    received = lax.all_to_all(copies, "z", split_axis=0, concat_axis=0, tiled=True)
    line_neg = received[:, 0:X].reshape(Z * X, embed_width)
    spread, line = call(
        spread_kernel,
        (
            jax.ShapeDtypeStruct((3, line_count, WIDE), bf16),
            jax.ShapeDtypeStruct((line_count, slot_count), jnp.int32),
        ),
        line_count * WIDE * 48,
        line_count * WIDE * 6,
        56,
        grid=(Z,),
        in_specs=[SMEM, pl.BlockSpec((1, 8, embed_width), lambda i: (i, 0, 0))],
        out_specs=(
            pl.BlockSpec((3, query_count, WIDE), lambda i: (0, i, 0)),
            pl.BlockSpec((query_count, slot_count), lambda i: (i, 0)),
        ),
    )(here, received)
    part = dot_nn(spread.reshape(3 * line_count, WIDE), plane).astype(bf16)
    part, plane, line, line_neg = lax.optimization_barrier((part, plane, line, line_neg))
    got = lax.psum_scatter(
        part.reshape(3, line_count, embed_width), "z", scatter_dimension=1, tiled=True
    )

    core_plane = lax.dynamic_index_in_dim(plane.reshape(Y, C, X, BLOCK, embed_width), c, axis=1, keepdims=False)
    core_plane = core_plane.transpose(1, 0, 2, 3)
    core_neg = core_plane[:, :, PART].reshape(X * Y, embed_width)
    core_plane = core_plane.reshape(NARROW, embed_width)
    some_neg = lax.all_gather(line_neg, "y", axis=0, tiled=True)
    other_neg = lax.ppermute(some_neg, "c", SIBLING)
    line_sib = lax.ppermute(line, "c", SIBLING)

    def node_weights(some_line):
        return call(
            node_weights_kernel,
            jax.ShapeDtypeStruct((3, NARROW, line_count), bf16),
            line_count * NARROW * 48,
            line_count * NARROW * 6,
            12,
            grid=(X,),
            in_specs=[SMEM, pl.BlockSpec((slot_count, line_count), lambda i: (0, 0))],
            out_specs=pl.BlockSpec((3, OWN, line_count), lambda i: (0, i, 0)),
        )(here, some_line.T)

    own_w, sib_w = node_weights(line), node_weights(line_sib)
    got, own_w, sib_w, core_plane, core_neg, some_neg, other_neg, my_pre = lax.optimization_barrier(
        (got, own_w, sib_w, core_plane, core_neg, some_neg, other_neg, my_pre)
    )

    payload_width = 2 * embed_width + 128
    payload = call(
        query_kernel,
        jax.ShapeDtypeStruct((query_count, payload_width), f32),
        4 * query_count * 512 * embed_width,
        1 << 20,
        10,
        in_specs=[VMEM] * 3,
        out_specs=VMEM,
    )(got, some_neg, other_neg)
    own = lax.all_gather(payload.astype(f16), "z", axis=0, tiled=True).astype(bf16)
    sib = lax.ppermute(own, "c", SIBLING)

    block = pl.BlockSpec((OWN, embed_width), lambda i: (i, 0))

    def node_side(weights, vectors, kind, *before):
        return call(
            node_grad_kernel,
            jax.ShapeDtypeStruct((NARROW, embed_width), kind),
            4 * line_count * NARROW * embed_width,
            10 << 20,
            28,
            grid=(X,),
            in_specs=[
                pl.BlockSpec((3, OWN, line_count), lambda i: (0, i, 0)),
                pl.BlockSpec((line_count, payload_width), lambda i: (0, 0)),
                block,
                pl.BlockSpec((X * Y, embed_width), lambda i: (0, 0)),
            ]
            + [block] * len(before),
            out_specs=block,
            scratch_shapes=[pltpu.VMEM((8, line_count), f32), pltpu.VMEM((X * Y, line_count), bf16)],
        )(weights, vectors, core_plane, core_neg, *before)

    node_grads = node_side(sib_w, sib, bf16, node_side(own_w, own, f32))

    pieces = lax.all_to_all(node_grads, ("x", "y"), split_axis=0, concat_axis=0, tiled=True)
    pre_grad = call(
        owner_kernel,
        jax.ShapeDtypeStruct((BLOCK, embed_width), bf16),
        1 << 22,
        3 << 20,
        10,
        in_specs=[VMEM] * 2,
        out_specs=VMEM,
    )(pieces.reshape(X * Y, BLOCK, embed_width), my_pre)
    all_pre_grad = lax.all_gather(pre_grad, "x", axis=0, tiled=True)
    return call(
        table_kernel,
        jax.ShapeDtypeStruct((ROWS, feat_width), f32),
        2 * OWN * embed_width * feat_width,
        4 << 20,
        16,
        in_specs=[SMEM, VMEM, VMEM],
        out_specs=VMEM,
    )(neg_row, all_pre_grad, projection)


def solution(mesh):
    grid = Mesh(mesh.devices.reshape(Y, Z, C, X), ("y", "z", "c", "x"))
    shard = ("y", "z", "c")
    every = ("y", "z", "c", "x")
    return jax.shard_map(
        on_device,
        mesh=grid,
        in_specs=(
            P(shard, None),
            P(),
            P(every, None, None),
            P(every, None),
            P(every, None),
            P(shard),
        ),
        out_specs=P(shard, None),
        check_vma=False,
    )
```

```python
import jax
import jax.numpy as jnp
from jax import lax
from jax.experimental import pallas as pl
from jax.experimental.pallas import tpu as pltpu
from jax.sharding import Mesh
from jax.sharding import PartitionSpec as P

score_scale = 8.0
margin_value = 0.1
epsilon = 1e-06
log_two = 0.6931471805599453

Y, Z, C, X = 4, 16, 2, 4
ROWS = 256
PART = ROWS // X
BLOCK = PART + 8
OWN = X * BLOCK
WIDE = Y * C * OWN
NARROW = Y * OWN
bf16 = jnp.bfloat16
f16 = jnp.float16
f32 = jnp.float32
SIBLING = [(0, 1), (1, 0)]


def silu_slope(preact):
    gate_value = jax.nn.sigmoid(preact)
    return gate_value * (1.0 + preact * (1.0 - gate_value))


def row_sum(values):
    return jnp.sum(values, axis=1, keepdims=True)


def row_norm(values):
    return jnp.sqrt(row_sum(values * values) + epsilon)


def weigh(score, positive):
    return (score_scale * jax.nn.sigmoid(score_scale * (score - positive + margin_value))).astype(bf16)


def dot_nn(left, right):
    return lax.dot_general(left, right, (((1,), (0,)), ((), ())), preferred_element_type=f32)


def dot_nt(left, right):
    return lax.dot_general(left, right, (((1,), (1,)), ((), ())), preferred_element_type=f32)


def decode(packed, axis):
    owner = packed & 127
    row = (packed >> 7) & 255
    visits = (packed >> 15).astype(f32)
    coefs = visits / jnp.sum(visits, axis=axis, keepdims=True)
    return owner >> 5, owner & 1, (owner >> 1) & 15, row >> 6, row & 63, coefs


def embed_kernel(neg_row_ref, table_hbm, projection_hbm, pre_ref, shared_ref, negs_ref, table_ref, projection_ref, sems):
    loads = (
        pltpu.make_async_copy(table_hbm, table_ref, sems.at[0]),
        pltpu.make_async_copy(projection_hbm, projection_ref, sems.at[1]),
    )
    for load in loads:
        load.start()
    picks = lax.broadcasted_iota(jnp.int32, (X * 8, ROWS), 0)
    cols = lax.broadcasted_iota(jnp.int32, (X * 8, ROWS), 1)
    hot = jnp.zeros((X * 8, ROWS), f32)
    for i in range(X):
        hot = hot + jnp.where((picks == 8 * i) & (cols == neg_row_ref[i]), 1.0, 0.0)
    for load in loads:
        load.wait()
    neg_rows = dot_nn(hot.astype(bf16), table_ref[...]).astype(bf16)
    neg_pre = dot_nn(neg_rows, projection_ref[...])
    neg_act = neg_pre * jax.nn.sigmoid(neg_pre)
    neg_unit = (neg_act / row_norm(neg_act)).astype(bf16)
    source = lax.broadcasted_iota(jnp.int32, (8, X * 8), 0) * 8
    pick = jnp.where(source == lax.broadcasted_iota(jnp.int32, (8, X * 8), 1), 1.0, 0.0)
    negs_ref[...] = dot_nn(pick.astype(bf16), neg_unit).astype(bf16)
    for i in range(X):
        node_pre = dot_nn(table_ref[i * PART : (i + 1) * PART], projection_ref[...])
        start = i * BLOCK
        pre_ref[start : start + PART] = node_pre
        pre_ref[start + PART : start + BLOCK] = neg_pre[8 * i : 8 * i + 8]
        shared_ref[start : start + PART] = (node_pre * jax.nn.sigmoid(node_pre)).astype(bf16)
        shared_ref[start + PART : start + BLOCK] = neg_unit[8 * i : 8 * i + 8]


def spread_kernel(where_ref, received_ref, out_ref, line_ref):
    rows, slots = line_ref.shape
    tiles = [received_ref[0, X:8, t * 128 : (t + 1) * 128].astype(f32) for t in range(8)]
    fields = jnp.concatenate(tiles, axis=0)
    packed = fields[:, 0:slots] + fields[:, slots : 2 * slots] * 128.0 + fields[:, 2 * slots : 3 * slots] * 32768.0
    packed = packed.astype(jnp.int32)
    line_ref[...] = packed
    ny, nc, nz, part, rest, coefs = decode(packed, 1)
    column = jnp.where(nz == where_ref[0], (ny * C + nc) * OWN + part * BLOCK + rest, -1)
    filler = jnp.full((rows, 128 - slots), -1, jnp.int32)
    names = jnp.concatenate([column, filler], axis=1)
    place = lax.broadcasted_iota(jnp.int32, (rows, slots), 1)
    weights = jnp.where(place == 0, 1.0, jnp.where(place > 2, coefs, 0.0))
    weights = jnp.concatenate([weights, filler.astype(f32) * 0.0], axis=1)
    merged = weights
    for shift in range(1, slots):
        same = pltpu.roll(names, shift, 1) == names
        merged = merged + jnp.where(same, pltpu.roll(weights, shift, 1), 0.0)
    chunk = WIDE // 3
    for k in range(3):
        lanes = lax.broadcasted_iota(jnp.int32, (rows, chunk), 1) + k * chunk
        total = jnp.where(lanes == names[:, 0:1], merged[:, 0:1], 0.0)
        for slot in range(3, slots):
            total = jnp.where(lanes == names[:, slot : slot + 1], merged[:, slot : slot + 1], total)
        span = pl.ds(k * chunk, chunk)
        out_ref[0, :, span] = total.astype(bf16)
        out_ref[1, :, span] = jnp.where(lanes == names[:, 1:2], 1.0, 0.0).astype(bf16)
        out_ref[2, :, span] = jnp.where(lanes == names[:, 2:3], 1.0, 0.0).astype(bf16)


def node_weights_kernel(where_ref, line_ref, out_ref):
    ny, nc, nz, part, rest, coefs = decode(line_ref[...], 0)
    here = (nz == where_ref[0]) & (nc == where_ref[1])
    column = jnp.where(here, part * (Y * BLOCK) + ny * BLOCK + rest, -1)
    slots, count = column.shape
    base = pl.program_id(0) * OWN
    chunk = 32
    for k in range(OWN // chunk):
        nodes = lax.broadcasted_iota(jnp.int32, (chunk, count), 0) + (base + k * chunk)
        total = jnp.where(nodes == column[0:1], 1.0, 0.0)
        for slot in range(3, slots):
            total = total + jnp.where(nodes == column[slot : slot + 1], coefs[slot : slot + 1], 0.0)
        span = pl.ds(k * chunk, chunk)
        out_ref[0, span, :] = total.astype(bf16)
        out_ref[1, span, :] = jnp.where(nodes == column[1:2], 1.0, 0.0).astype(bf16)
        out_ref[2, span, :] = jnp.where(nodes == column[2:3], 1.0, 0.0).astype(bf16)


def query_kernel(got_ref, neg_a_ref, neg_b_ref, out_ref):
    count, width = got_ref.shape[1:]
    hood = got_ref[0].astype(f32)
    query_norm = row_norm(hood)
    query_unit = hood / query_norm
    query_embed = query_unit.astype(bf16)
    query_float = query_embed.astype(f32)
    first = got_ref[1].astype(f32)
    second = got_ref[2].astype(f32)
    first_norm, second_norm = row_norm(first), row_norm(second)
    first_embed = (first / first_norm).astype(bf16).astype(f32)
    second_embed = (second / second_norm).astype(bf16).astype(f32)
    positive = row_sum(query_float * first_embed)
    hard = weigh(row_sum(query_float * second_embed), positive).astype(f32)
    weight_a = weigh(dot_nt(query_embed, neg_a_ref[...]), positive)
    weight_b = weigh(dot_nt(query_embed, neg_b_ref[...]), positive)
    total = row_sum(weight_a.astype(f32)) + row_sum(weight_b.astype(f32)) + hard
    grad = dot_nn(weight_a, neg_a_ref[...]) + dot_nn(weight_b, neg_b_ref[...]) + hard * second_embed - total * first_embed
    grad = grad - query_unit * row_sum(query_unit * grad)
    power = jnp.exp(jnp.ceil(jnp.log(query_norm) * (1.0 / log_two)) * log_two).astype(bf16).astype(f32)
    inverse = (16.0 / power).astype(bf16).astype(f32)
    out_ref[:, 0:width] = grad * (power / query_norm)
    out_ref[:, width : 2 * width] = query_float
    lanes = lax.broadcasted_iota(jnp.int32, (count, 128), 1)
    scalars = jnp.where(lanes == 0, inverse, 0.0)
    for place, value in ((1, total), (3, hard), (5, first_norm), (7, second_norm), (9, positive)):
        high = value.astype(bf16).astype(f32)
        scalars = jnp.where(lanes == place, high, scalars)
        scalars = jnp.where(lanes == place + 1, value - high, scalars)
    out_ref[:, 2 * width :] = scalars


def node_grad_kernel(*refs):
    weight_ref, ref, plane_ref, neg_ref = refs[:4]
    out_ref, row_ref, neg_w_ref = refs[-3:]
    step = pl.program_id(0)
    width = plane_ref.shape[1]

    @pl.when(step == 0)
    def _():
        scalars = ref[:, 2 * width :].astype(f32).T
        total = scalars[1:2] + scalars[2:3]
        hard = scalars[3:4] + scalars[4:5]
        row_ref[0:1] = scalars[0:1] * 0.0625
        row_ref[1:2] = -total / (scalars[5:6] + scalars[6:7])
        row_ref[2:3] = hard / (scalars[7:8] + scalars[8:9])
        scores = dot_nt(neg_ref[...], ref[:, width : 2 * width])
        neg_w_ref[...] = weigh(scores, scalars[9:10] + scalars[10:11])

    negs = neg_ref.shape[0]
    rows = lax.broadcasted_iota(jnp.int32, (OWN, negs), 0) + step * OWN
    spot = jnp.where(rows == lax.broadcasted_iota(jnp.int32, (OWN, negs), 1) * BLOCK + PART, 1.0, 0.0).astype(bf16)
    w_hood = (weight_ref[0].astype(f32) * row_ref[0:1]).astype(bf16)
    hood_part = dot_nn(w_hood, ref[:, 0:width])
    w_query = weight_ref[1].astype(f32) * row_ref[1:2] + weight_ref[2].astype(f32) * row_ref[2:3]
    w_query = (w_query + dot_nn(spot, neg_w_ref[...])).astype(bf16)
    query_part = dot_nn(w_query, ref[:, width : 2 * width])
    plane = plane_ref[...].astype(f32)
    place = lax.broadcasted_iota(jnp.int32, (OWN, 1), 0) % BLOCK
    inverse = jnp.where(place == PART, 0.0, 1.0 / (row_sum(plane * plane) + epsilon))
    query_part = query_part - plane * (inverse * row_sum(plane * query_part))
    result = hood_part + query_part
    if len(refs) > 7:
        result = result + refs[4][...]
    out_ref[...] = result.astype(out_ref.dtype)


def owner_kernel(pieces_ref, pre_ref, out_ref):
    total = pieces_ref[0].astype(f32)
    for k in range(1, pieces_ref.shape[0]):
        total = total + pieces_ref[k].astype(f32)
    pre = pre_ref[...]
    act = pre * jax.nn.sigmoid(pre)
    norm = row_norm(act)
    unit = act / norm
    place = lax.broadcasted_iota(jnp.int32, (BLOCK, 1), 0)
    back = (total - unit * row_sum(unit * total)) / norm
    total = jnp.where(place == PART, back, total)
    out_ref[...] = (total * silu_slope(pre)).astype(bf16)


def table_kernel(neg_row_ref, grad_ref, projection_ref, out_ref):
    out = dot_nt(grad_ref[...], projection_ref[...])
    rows = lax.broadcasted_iota(jnp.int32, (PART, 1), 0)
    for k in range(X):
        block = out[k * BLOCK : k * BLOCK + PART]
        for i in range(X):
            hit = rows + k * PART == neg_row_ref[i]
            block = block + jnp.where(hit, out[i * BLOCK + PART : i * BLOCK + PART + 1], 0.0)
        out_ref[k * PART : (k + 1) * PART] = block


def call(kernel, out_shape, flops, moved, room, **rest):
    return pl.pallas_call(
        kernel,
        out_shape=out_shape,
        cost_estimate=pl.CostEstimate(flops=flops, bytes_accessed=moved, transcendentals=0),
        compiler_params=pltpu.CompilerParams(vmem_limit_bytes=room << 20),
        **rest,
    )


VMEM = pl.BlockSpec(memory_space=pltpu.VMEM)
SMEM = pl.BlockSpec(memory_space=pltpu.SMEM)


def on_device(feature_table, projection, slot_owner, slot_row, visits, neg_row):
    z, c, x = (lax.axis_index(a) for a in ("z", "c", "x"))
    here = jnp.stack([z, c]).astype(jnp.int32)
    query_count, slot_count = slot_row.shape
    feat_width, embed_width = projection.shape
    line_count = Z * query_count

    pre, shared, negs = call(
        embed_kernel,
        (
            jax.ShapeDtypeStruct((OWN, embed_width), f32),
            jax.ShapeDtypeStruct((OWN, embed_width), bf16),
            jax.ShapeDtypeStruct((8, embed_width), bf16),
        ),
        2 * OWN * embed_width * feat_width,
        5 << 20,
        56,
        in_specs=[SMEM, pl.BlockSpec(memory_space=pl.ANY), pl.BlockSpec(memory_space=pl.ANY)],
        out_specs=(VMEM, VMEM, VMEM),
        scratch_shapes=[
            pltpu.VMEM((ROWS, feat_width), bf16),
            pltpu.VMEM((feat_width, embed_width), bf16),
            pltpu.SemaphoreType.DMA((2,)),
        ],
    )(neg_row, feature_table, projection)
    plane = lax.all_gather(shared, ("y", "c"), axis=0, tiled=True)
    my_pre = lax.dynamic_slice_in_dim(pre, x * BLOCK, BLOCK, axis=0)

    shifted = jnp.pad(visits, ((0, 0), (3, 0)))
    fields = jnp.concatenate([slot_owner.reshape(query_count, slot_count), slot_row, shifted], axis=1)
    fields = jnp.pad(fields.astype(bf16), ((0, 0), (0, 128 - 3 * slot_count)))
    fields = fields.reshape(8, 4, 128).transpose(1, 0, 2).reshape(4, embed_width)
    block = jnp.concatenate([negs[0:X], fields], axis=0)
    copies = jnp.broadcast_to(block, (Z, 8, embed_width))
    received = lax.all_to_all(copies, "z", split_axis=0, concat_axis=0, tiled=True)
    line_neg = received[:, 0:X].reshape(Z * X, embed_width)
    spread, line = call(
        spread_kernel,
        (
            jax.ShapeDtypeStruct((3, line_count, WIDE), bf16),
            jax.ShapeDtypeStruct((line_count, slot_count), jnp.int32),
        ),
        line_count * WIDE * 48,
        line_count * WIDE * 6,
        56,
        grid=(Z,),
        in_specs=[SMEM, pl.BlockSpec((1, 8, embed_width), lambda i: (i, 0, 0))],
        out_specs=(
            pl.BlockSpec((3, query_count, WIDE), lambda i: (0, i, 0)),
            pl.BlockSpec((query_count, slot_count), lambda i: (i, 0)),
        ),
    )(here, received)
    part = dot_nn(spread.reshape(3 * line_count, WIDE), plane).astype(bf16)
    part, plane, line, line_neg = lax.optimization_barrier((part, plane, line, line_neg))
    got = lax.psum_scatter(
        part.reshape(3, line_count, embed_width), "z", scatter_dimension=1, tiled=True
    )

    core_plane = lax.dynamic_index_in_dim(plane.reshape(Y, C, X, BLOCK, embed_width), c, axis=1, keepdims=False)
    core_plane = core_plane.transpose(1, 0, 2, 3)
    core_neg = core_plane[:, :, PART].reshape(X * Y, embed_width)
    core_plane = core_plane.reshape(NARROW, embed_width)
    some_neg = lax.all_gather(line_neg, "y", axis=0, tiled=True)
    other_neg = lax.ppermute(some_neg, "c", SIBLING)
    line_sib = lax.ppermute(line, "c", SIBLING)

    def node_weights(some_line):
        return call(
            node_weights_kernel,
            jax.ShapeDtypeStruct((3, NARROW, line_count), bf16),
            line_count * NARROW * 48,
            line_count * NARROW * 6,
            12,
            grid=(X,),
            in_specs=[SMEM, pl.BlockSpec((slot_count, line_count), lambda i: (0, 0))],
            out_specs=pl.BlockSpec((3, OWN, line_count), lambda i: (0, i, 0)),
        )(here, some_line.T)

    own_w, sib_w = node_weights(line), node_weights(line_sib)
    got, own_w, sib_w, core_plane, core_neg, some_neg, other_neg, my_pre = lax.optimization_barrier(
        (got, own_w, sib_w, core_plane, core_neg, some_neg, other_neg, my_pre)
    )

    payload_width = 2 * embed_width + 128
    payload = call(
        query_kernel,
        jax.ShapeDtypeStruct((query_count, payload_width), f32),
        4 * query_count * 512 * embed_width,
        1 << 20,
        10,
        in_specs=[VMEM] * 3,
        out_specs=VMEM,
    )(got, some_neg, other_neg)
    own = lax.all_gather(payload.astype(f16), "z", axis=0, tiled=True).astype(bf16)
    sib = lax.ppermute(own, "c", SIBLING)

    block = pl.BlockSpec((OWN, embed_width), lambda i: (i, 0))

    def node_side(weights, vectors, kind, *before):
        return call(
            node_grad_kernel,
            jax.ShapeDtypeStruct((NARROW, embed_width), kind),
            4 * line_count * NARROW * embed_width,
            10 << 20,
            28,
            grid=(X,),
            in_specs=[
                pl.BlockSpec((3, OWN, line_count), lambda i: (0, i, 0)),
                pl.BlockSpec((line_count, payload_width), lambda i: (0, 0)),
                block,
                pl.BlockSpec((X * Y, embed_width), lambda i: (0, 0)),
            ]
            + [block] * len(before),
            out_specs=block,
            scratch_shapes=[pltpu.VMEM((8, line_count), f32), pltpu.VMEM((X * Y, line_count), bf16)],
        )(weights, vectors, core_plane, core_neg, *before)

    node_grads = node_side(sib_w, sib, bf16, node_side(own_w, own, f32))

    pieces = lax.all_to_all(node_grads, ("x", "y"), split_axis=0, concat_axis=0, tiled=True)
    pre_grad = call(
        owner_kernel,
        jax.ShapeDtypeStruct((BLOCK, embed_width), bf16),
        1 << 22,
        3 << 20,
        10,
        in_specs=[VMEM] * 2,
        out_specs=VMEM,
    )(pieces.reshape(X * Y, BLOCK, embed_width), my_pre)
    all_pre_grad = lax.all_gather(pre_grad, "x", axis=0, tiled=True)
    return call(
        table_kernel,
        jax.ShapeDtypeStruct((ROWS, feat_width), f32),
        2 * OWN * embed_width * feat_width,
        4 << 20,
        16,
        in_specs=[SMEM, VMEM, VMEM],
        out_specs=VMEM,
    )(neg_row, all_pre_grad, projection)


def solution(mesh):
    grid = Mesh(mesh.devices.reshape(Y, Z, C, X), ("y", "z", "c", "x"))
    shard = ("y", "z", "c")
    every = ("y", "z", "c", "x")
    return jax.shard_map(
        on_device,
        mesh=grid,
        in_specs=(
            P(shard, None),
            P(),
            P(every, None, None),
            P(every, None),
            P(every, None),
            P(shard),
        ),
        out_specs=P(shard, None),
        check_vma=False,
    )
```

```python
import jax
import jax.numpy as jnp
from jax import lax
from jax.experimental import pallas as pl
from jax.experimental.pallas import tpu as pltpu
from jax.sharding import Mesh
from jax.sharding import PartitionSpec as P

score_scale = 8.0
margin_value = 0.1
epsilon = 1e-06
log_two = 0.6931471805599453

Y, Z, C, X = 4, 16, 2, 4
ROWS = 256
PART = ROWS // X
BLOCK = PART + 8
OWN = X * BLOCK
WIDE = Y * C * OWN
NARROW = Y * OWN
bf16 = jnp.bfloat16
f16 = jnp.float16
f32 = jnp.float32
SIBLING = [(0, 1), (1, 0)]


def silu_slope(preact):
    gate_value = jax.nn.sigmoid(preact)
    return gate_value * (1.0 + preact * (1.0 - gate_value))


def row_sum(values):
    return jnp.sum(values, axis=1, keepdims=True)


def row_norm(values):
    return jnp.sqrt(row_sum(values * values) + epsilon)


def weigh(score, positive):
    return (score_scale * jax.nn.sigmoid(score_scale * (score - positive + margin_value))).astype(bf16)


def dot_nn(left, right):
    return lax.dot_general(left, right, (((1,), (0,)), ((), ())), preferred_element_type=f32)


def dot_nt(left, right):
    return lax.dot_general(left, right, (((1,), (1,)), ((), ())), preferred_element_type=f32)


def decode(packed, axis):
    owner = packed & 127
    row = (packed >> 7) & 255
    visits = (packed >> 15).astype(f32)
    coefs = visits / jnp.sum(visits, axis=axis, keepdims=True)
    return owner >> 5, owner & 1, (owner >> 1) & 15, row >> 6, row & 63, coefs


def embed_kernel(neg_row_ref, table_hbm, projection_hbm, pre_ref, shared_ref, negs_ref, table_ref, projection_ref, sems):
    loads = (
        pltpu.make_async_copy(table_hbm, table_ref, sems.at[0]),
        pltpu.make_async_copy(projection_hbm, projection_ref, sems.at[1]),
    )
    for load in loads:
        load.start()
    picks = lax.broadcasted_iota(jnp.int32, (X * 8, ROWS), 0)
    cols = lax.broadcasted_iota(jnp.int32, (X * 8, ROWS), 1)
    hot = jnp.zeros((X * 8, ROWS), f32)
    for i in range(X):
        hot = hot + jnp.where((picks == 8 * i) & (cols == neg_row_ref[i]), 1.0, 0.0)
    for load in loads:
        load.wait()
    neg_rows = dot_nn(hot.astype(bf16), table_ref[...]).astype(bf16)
    neg_pre = dot_nn(neg_rows, projection_ref[...])
    neg_act = neg_pre * jax.nn.sigmoid(neg_pre)
    neg_unit = (neg_act / row_norm(neg_act)).astype(bf16)
    source = lax.broadcasted_iota(jnp.int32, (8, X * 8), 0) * 8
    pick = jnp.where(source == lax.broadcasted_iota(jnp.int32, (8, X * 8), 1), 1.0, 0.0)
    negs_ref[...] = dot_nn(pick.astype(bf16), neg_unit).astype(bf16)
    for i in range(X):
        node_pre = dot_nn(table_ref[i * PART : (i + 1) * PART], projection_ref[...])
        start = i * BLOCK
        pre_ref[start : start + PART] = node_pre
        pre_ref[start + PART : start + BLOCK] = neg_pre[8 * i : 8 * i + 8]
        shared_ref[start : start + PART] = (node_pre * jax.nn.sigmoid(node_pre)).astype(bf16)
        shared_ref[start + PART : start + BLOCK] = neg_unit[8 * i : 8 * i + 8]


def spread_kernel(where_ref, received_ref, out_ref, line_ref):
    rows, slots = line_ref.shape
    tiles = [received_ref[0, X:8, t * 128 : (t + 1) * 128].astype(f32) for t in range(8)]
    fields = jnp.concatenate(tiles, axis=0)
    packed = fields[:, 0:slots] + fields[:, slots : 2 * slots] * 128.0 + fields[:, 2 * slots : 3 * slots] * 32768.0
    packed = packed.astype(jnp.int32)
    line_ref[...] = packed
    ny, nc, nz, part, rest, coefs = decode(packed, 1)
    column = jnp.where(nz == where_ref[0], (ny * C + nc) * OWN + part * BLOCK + rest, -1)
    chunk = WIDE // 3
    for k in range(3):
        lanes = lax.broadcasted_iota(jnp.int32, (rows, chunk), 1) + k * chunk
        total = jnp.where(lanes == column[:, 0:1], 1.0, 0.0)
        for slot in range(3, slots):
            total = total + jnp.where(lanes == column[:, slot : slot + 1], coefs[:, slot : slot + 1], 0.0)
        span = pl.ds(k * chunk, chunk)
        out_ref[0, :, span] = total.astype(bf16)
        out_ref[1, :, span] = jnp.where(lanes == column[:, 1:2], 1.0, 0.0).astype(bf16)
        out_ref[2, :, span] = jnp.where(lanes == column[:, 2:3], 1.0, 0.0).astype(bf16)


def node_weights_kernel(where_ref, line_ref, out_ref):
    ny, nc, nz, part, rest, coefs = decode(line_ref[...], 0)
    here = (nz == where_ref[0]) & (nc == where_ref[1])
    column = jnp.where(here, part * (Y * BLOCK) + ny * BLOCK + rest, -1)
    slots, count = column.shape
    base = pl.program_id(0) * OWN
    chunk = 32
    for k in range(OWN // chunk):
        nodes = lax.broadcasted_iota(jnp.int32, (chunk, count), 0) + (base + k * chunk)
        total = jnp.where(nodes == column[0:1], 1.0, 0.0)
        for slot in range(3, slots):
            total = total + jnp.where(nodes == column[slot : slot + 1], coefs[slot : slot + 1], 0.0)
        span = pl.ds(k * chunk, chunk)
        out_ref[0, span, :] = total.astype(bf16)
        out_ref[1, span, :] = jnp.where(nodes == column[1:2], 1.0, 0.0).astype(bf16)
        out_ref[2, span, :] = jnp.where(nodes == column[2:3], 1.0, 0.0).astype(bf16)


def query_kernel(got_ref, neg_a_ref, neg_b_ref, out_ref):
    count, width = got_ref.shape[1:]
    hood = got_ref[0].astype(f32)
    query_norm = row_norm(hood)
    query_unit = hood / query_norm
    query_embed = query_unit.astype(bf16)
    query_float = query_embed.astype(f32)
    first = got_ref[1].astype(f32)
    second = got_ref[2].astype(f32)
    first_norm, second_norm = row_norm(first), row_norm(second)
    first_embed = (first / first_norm).astype(bf16).astype(f32)
    second_embed = (second / second_norm).astype(bf16).astype(f32)
    positive = row_sum(query_float * first_embed)
    hard = weigh(row_sum(query_float * second_embed), positive).astype(f32)
    weight_a = weigh(dot_nt(query_embed, neg_a_ref[...]), positive)
    weight_b = weigh(dot_nt(query_embed, neg_b_ref[...]), positive)
    total = row_sum(weight_a.astype(f32)) + row_sum(weight_b.astype(f32)) + hard
    grad = dot_nn(weight_a, neg_a_ref[...]) + dot_nn(weight_b, neg_b_ref[...]) + hard * second_embed - total * first_embed
    grad = grad - query_unit * row_sum(query_unit * grad)
    power = jnp.exp(jnp.ceil(jnp.log(query_norm) * (1.0 / log_two)) * log_two).astype(bf16).astype(f32)
    inverse = (16.0 / power).astype(bf16).astype(f32)
    out_ref[:, 0:width] = grad * (power / query_norm)
    out_ref[:, width : 2 * width] = query_float
    lanes = lax.broadcasted_iota(jnp.int32, (count, 128), 1)
    scalars = jnp.where(lanes == 0, inverse, 0.0)
    for place, value in ((1, total), (3, hard), (5, first_norm), (7, second_norm), (9, positive)):
        high = value.astype(bf16).astype(f32)
        scalars = jnp.where(lanes == place, high, scalars)
        scalars = jnp.where(lanes == place + 1, value - high, scalars)
    out_ref[:, 2 * width :] = scalars


def node_grad_kernel(*refs):
    weight_ref, ref, plane_ref, neg_ref = refs[:4]
    out_ref, row_ref, neg_w_ref = refs[-3:]
    step = pl.program_id(0)
    width = plane_ref.shape[1]

    @pl.when(step == 0)
    def _():
        scalars = ref[:, 2 * width :].astype(f32).T
        total = scalars[1:2] + scalars[2:3]
        hard = scalars[3:4] + scalars[4:5]
        row_ref[0:1] = scalars[0:1] * 0.0625
        row_ref[1:2] = -total / (scalars[5:6] + scalars[6:7])
        row_ref[2:3] = hard / (scalars[7:8] + scalars[8:9])
        scores = dot_nt(neg_ref[...], ref[:, width : 2 * width])
        neg_w_ref[...] = weigh(scores, scalars[9:10] + scalars[10:11])

    negs = neg_ref.shape[0]
    rows = lax.broadcasted_iota(jnp.int32, (OWN, negs), 0) + step * OWN
    spot = jnp.where(rows == lax.broadcasted_iota(jnp.int32, (OWN, negs), 1) * BLOCK + PART, 1.0, 0.0).astype(bf16)
    w_hood = (weight_ref[0].astype(f32) * row_ref[0:1]).astype(bf16)
    hood_part = dot_nn(w_hood, ref[:, 0:width])
    w_query = weight_ref[1].astype(f32) * row_ref[1:2] + weight_ref[2].astype(f32) * row_ref[2:3]
    w_query = (w_query + dot_nn(spot, neg_w_ref[...])).astype(bf16)
    query_part = dot_nn(w_query, ref[:, width : 2 * width])
    plane = plane_ref[...].astype(f32)
    place = lax.broadcasted_iota(jnp.int32, (OWN, 1), 0) % BLOCK
    inverse = jnp.where(place == PART, 0.0, 1.0 / (row_sum(plane * plane) + epsilon))
    query_part = query_part - plane * (inverse * row_sum(plane * query_part))
    result = hood_part + query_part
    if len(refs) > 7:
        result = result + refs[4][...]
    out_ref[...] = result.astype(out_ref.dtype)


def owner_kernel(pieces_ref, pre_ref, out_ref):
    total = pieces_ref[0].astype(f32)
    for k in range(1, pieces_ref.shape[0]):
        total = total + pieces_ref[k].astype(f32)
    pre = pre_ref[...]
    act = pre * jax.nn.sigmoid(pre)
    norm = row_norm(act)
    unit = act / norm
    place = lax.broadcasted_iota(jnp.int32, (BLOCK, 1), 0)
    back = (total - unit * row_sum(unit * total)) / norm
    total = jnp.where(place == PART, back, total)
    out_ref[...] = (total * silu_slope(pre)).astype(bf16)


def table_kernel(neg_row_ref, grad_ref, projection_ref, out_ref):
    out = dot_nt(grad_ref[...], projection_ref[...])
    rows = lax.broadcasted_iota(jnp.int32, (PART, 1), 0)
    for k in range(X):
        block = out[k * BLOCK : k * BLOCK + PART]
        for i in range(X):
            hit = rows + k * PART == neg_row_ref[i]
            block = block + jnp.where(hit, out[i * BLOCK + PART : i * BLOCK + PART + 1], 0.0)
        out_ref[k * PART : (k + 1) * PART] = block


def call(kernel, out_shape, flops, moved, room, **rest):
    return pl.pallas_call(
        kernel,
        out_shape=out_shape,
        cost_estimate=pl.CostEstimate(flops=flops, bytes_accessed=moved, transcendentals=0),
        compiler_params=pltpu.CompilerParams(vmem_limit_bytes=room << 20),
        **rest,
    )


VMEM = pl.BlockSpec(memory_space=pltpu.VMEM)
SMEM = pl.BlockSpec(memory_space=pltpu.SMEM)


def on_device(feature_table, projection, slot_owner, slot_row, visits, neg_row):
    z, c, x = (lax.axis_index(a) for a in ("z", "c", "x"))
    here = jnp.stack([z, c]).astype(jnp.int32)
    query_count, slot_count = slot_row.shape
    feat_width, embed_width = projection.shape
    line_count = Z * query_count

    pre, shared, negs = call(
        embed_kernel,
        (
            jax.ShapeDtypeStruct((OWN, embed_width), f32),
            jax.ShapeDtypeStruct((OWN, embed_width), bf16),
            jax.ShapeDtypeStruct((8, embed_width), bf16),
        ),
        2 * OWN * embed_width * feat_width,
        5 << 20,
        56,
        in_specs=[SMEM, pl.BlockSpec(memory_space=pl.ANY), pl.BlockSpec(memory_space=pl.ANY)],
        out_specs=(VMEM, VMEM, VMEM),
        scratch_shapes=[
            pltpu.VMEM((ROWS, feat_width), bf16),
            pltpu.VMEM((feat_width, embed_width), bf16),
            pltpu.SemaphoreType.DMA((2,)),
        ],
    )(neg_row, feature_table, projection)
    plane = lax.all_gather(shared, ("y", "c"), axis=0, tiled=True)
    my_pre = lax.dynamic_slice_in_dim(pre, x * BLOCK, BLOCK, axis=0)

    shifted = jnp.pad(visits, ((0, 0), (3, 0)))
    fields = jnp.concatenate([slot_owner.reshape(query_count, slot_count), slot_row, shifted], axis=1)
    fields = jnp.pad(fields.astype(bf16), ((0, 0), (0, 128 - 3 * slot_count)))
    fields = fields.reshape(8, 4, 128).transpose(1, 0, 2).reshape(4, embed_width)
    block = jnp.concatenate([negs[0:X], fields], axis=0)
    copies = jnp.broadcast_to(block, (Z, 8, embed_width))
    received = lax.all_to_all(copies, "z", split_axis=0, concat_axis=0, tiled=True)
    line_neg = received[:, 0:X].reshape(Z * X, embed_width)
    spread, line = call(
        spread_kernel,
        (
            jax.ShapeDtypeStruct((3, line_count, WIDE), bf16),
            jax.ShapeDtypeStruct((line_count, slot_count), jnp.int32),
        ),
        line_count * WIDE * 48,
        line_count * WIDE * 6,
        56,
        grid=(Z,),
        in_specs=[SMEM, pl.BlockSpec((1, 8, embed_width), lambda i: (i, 0, 0))],
        out_specs=(
            pl.BlockSpec((3, query_count, WIDE), lambda i: (0, i, 0)),
            pl.BlockSpec((query_count, slot_count), lambda i: (i, 0)),
        ),
    )(here, received)
    part = dot_nn(spread.reshape(3 * line_count, WIDE), plane).astype(bf16)
    part, plane, line, line_neg = lax.optimization_barrier((part, plane, line, line_neg))
    got = lax.psum_scatter(
        part.reshape(3, line_count, embed_width), "z", scatter_dimension=1, tiled=True
    )

    core_plane = lax.dynamic_index_in_dim(plane.reshape(Y, C, X, BLOCK, embed_width), c, axis=1, keepdims=False)
    core_plane = core_plane.transpose(1, 0, 2, 3)
    core_neg = core_plane[:, :, PART].reshape(X * Y, embed_width)
    core_plane = core_plane.reshape(NARROW, embed_width)
    some_neg = lax.all_gather(line_neg, "y", axis=0, tiled=True)
    other_neg = lax.ppermute(some_neg, "c", SIBLING)
    line_sib = lax.ppermute(line, "c", SIBLING)

    def node_weights(some_line):
        return call(
            node_weights_kernel,
            jax.ShapeDtypeStruct((3, NARROW, line_count), bf16),
            line_count * NARROW * 48,
            line_count * NARROW * 6,
            12,
            grid=(X,),
            in_specs=[SMEM, pl.BlockSpec((slot_count, line_count), lambda i: (0, 0))],
            out_specs=pl.BlockSpec((3, OWN, line_count), lambda i: (0, i, 0)),
        )(here, some_line.T)

    own_w, sib_w = node_weights(line), node_weights(line_sib)
    got, own_w, sib_w, core_plane, core_neg, some_neg, other_neg, my_pre = lax.optimization_barrier(
        (got, own_w, sib_w, core_plane, core_neg, some_neg, other_neg, my_pre)
    )

    payload_width = 2 * embed_width + 128
    payload = call(
        query_kernel,
        jax.ShapeDtypeStruct((query_count, payload_width), f32),
        4 * query_count * 512 * embed_width,
        1 << 20,
        10,
        in_specs=[VMEM] * 3,
        out_specs=VMEM,
    )(got, some_neg, other_neg)
    own = lax.all_gather(payload.astype(f16), "z", axis=0, tiled=True).astype(bf16)
    sib = lax.ppermute(own, "c", SIBLING)

    block = pl.BlockSpec((OWN, embed_width), lambda i: (i, 0))

    def node_side(weights, vectors, kind, *before):
        return call(
            node_grad_kernel,
            jax.ShapeDtypeStruct((NARROW, embed_width), kind),
            4 * line_count * NARROW * embed_width,
            10 << 20,
            28,
            grid=(X,),
            in_specs=[
                pl.BlockSpec((3, OWN, line_count), lambda i: (0, i, 0)),
                pl.BlockSpec((line_count, payload_width), lambda i: (0, 0)),
                block,
                pl.BlockSpec((X * Y, embed_width), lambda i: (0, 0)),
            ]
            + [block] * len(before),
            out_specs=block,
            scratch_shapes=[pltpu.VMEM((8, line_count), f32), pltpu.VMEM((X * Y, line_count), bf16)],
        )(weights, vectors, core_plane, core_neg, *before)

    node_grads = node_side(sib_w, sib, bf16, node_side(own_w, own, f32))

    pieces = lax.all_to_all(node_grads, ("x", "y"), split_axis=0, concat_axis=0, tiled=True)
    pre_grad = call(
        owner_kernel,
        jax.ShapeDtypeStruct((BLOCK, embed_width), bf16),
        1 << 22,
        3 << 20,
        10,
        in_specs=[VMEM] * 2,
        out_specs=VMEM,
    )(pieces.reshape(X * Y, BLOCK, embed_width), my_pre)
    all_pre_grad = lax.all_gather(pre_grad, "x", axis=0, tiled=True)
    return call(
        table_kernel,
        jax.ShapeDtypeStruct((ROWS, feat_width), f32),
        2 * OWN * embed_width * feat_width,
        4 << 20,
        16,
        in_specs=[SMEM, VMEM, VMEM],
        out_specs=VMEM,
    )(neg_row, all_pre_grad, projection)


def solution(mesh):
    grid = Mesh(mesh.devices.reshape(Y, Z, C, X), ("y", "z", "c", "x"))
    shard = ("y", "z", "c")
    every = ("y", "z", "c", "x")
    return jax.shard_map(
        on_device,
        mesh=grid,
        in_specs=(
            P(shard, None),
            P(),
            P(every, None, None),
            P(every, None),
            P(every, None),
            P(shard),
        ),
        out_specs=P(shard, None),
        check_vma=False,
    )
```
